256 devices in a mesh: dp: 16 (over z_hi, y, core), tensor: 16 (over x, z_lo).
Axes of the slice: x: 4, y: 4, z: 8 (z_hi: 2, z_lo: 4; z = z_hi * 4 + z_lo), core: 2. Of those that a mesh axis runs over, the one named last changes fastest.
Arguments:
- tokens: bfloat16 [2048, 1024], P('dp', 'tensor'), may hold values from -6 to 6
- init_noise: float32 [2048, 1024], P('dp', 'tensor'), may hold values from -1 to 1
- segment_ids: int32 [2048], P('dp'), may hold values from 0 to 31, never falling along the last dimension, each value on 1 to 256 neighbouring positions
- target: float32 [2048, 1024], P('dp', 'tensor'), may hold values from -6 to 6
- norm_gain: float32 [1024], replicated, may hold values from 0.1 to 1.9
- weight_in: bfloat16 [1024, 32768], P(None, 'tensor'), may hold values from -0.1875 to 0.1875
- weight_out: bfloat16 [32768, 1024], P('tensor'), may hold values from -0.03125 to 0.03125
- moment_in: float32 [1024, 32768], P('dp', 'tensor'), may hold values from -1.5 to 1.5
- moment_out: float32 [32768, 1024], P('tensor', 'dp'), may hold values from -1.5 to 1.5
Outputs:
- new_weight_in: bfloat16 [1024, 32768], P('dp', 'tensor')
- new_weight_out: bfloat16 [32768, 1024], P('tensor', 'dp')
- new_moment_in: float32 [1024, 32768], P('dp', 'tensor')
- new_moment_out: float32 [32768, 1024], P('tensor', 'dp')
- perturbation: float32 [2048, 1024], P('dp', 'tensor')
The draws below stay inside these ranges and needn't reach their ends.
Inputs may be any that keep to these rules, and one draw needn't show every extreme that they name: `segment_ids`: example ids never fall along the tokens; every example holds 1 to 256 tokens.
All inputs are finite; a program needn't handle non-finite values.
Results may differ from the reference program's by a relative error of at most 0.0051.
Values may be sent and summed in bfloat16 or wider, within the bound.
No kernel may reach another device: no remote copies, remote signals or barrier semaphores. Data moves between devices by JAX's collectives and lax.ppermute only.
A program may use at most 128 MiB of HBM per device.

```python
import math
import jax
import jax.numpy as jnp
import numpy as np
from jax import lax

D = 1024
FF = 32768
ASCENTS = 2
TOKENS = 2048
EXAMPLES = 32
MOST = 256
N_TENSOR = 16


def shard_levels(key, shape, cuts, least, high):
    def one(axis_at, blocks):
        steps = jax.random.uniform(jax.random.fold_in(jax.random.fold_in(key, 6), axis_at), (blocks,), jnp.float32, least / len(cuts), high / len(cuts))
        return jnp.repeat(jnp.exp(steps), shape[axis_at] // blocks).reshape((-1,) + (1,) * (len(shape) - axis_at - 1))

    gain = one(*cuts[0])
    for cut in cuts[1:]:
        gain = gain * one(*cut)
    return gain


def length_profile(number_of, total, limit, skew):
    weights = [(1 << 20) // math.isqrt(grade ** skew) + 1 for grade in range(2, number_of + 1)]
    surplus, given = total - limit - (number_of - 1), [1] * (number_of - 1)
    while surplus > 0:
        movable = [i for i in range(number_of - 1) if given[i] < limit]
        whole, remaining = sum([weights[i] for i in movable]), surplus
        for i in movable:
            more = min(limit - given[i], max(1, remaining * weights[i] // whole), surplus)
            given[i] = given[i] + more
            surplus = surplus - more
    return np.array([limit] + given)


def uneven(own_key, count, total, most, slope):
    if count == 2:
        one = jax.random.randint(own_key, (), max(1, total - most), min(most, total - 1) + 1)
        return jnp.stack([one, total - one])
    sizes = jnp.asarray(length_profile(count, total, most, slope), jnp.int32)
    couples = (count - 1) // 2
    giver, taker = sizes[1:1 + 2 * couples:2], sizes[2:2 + 2 * couples:2]
    room = jnp.minimum(giver - 1, most - taker)
    shifted = jax.random.randint(jax.random.fold_in(own_key, 1), (couples,), 0, 1 << 20) % (room + 1)
    sizes = sizes.at[1:1 + 2 * couples:2].set(giver - shifted).at[2:2 + 2 * couples:2].set(taker + shifted)
    return sizes[jax.random.permutation(jax.random.fold_in(own_key, 2), count)]


def scatter_about(stream_key, shape, width, most, pieces=(), held_as=jnp.bfloat16):
    gain = shard_levels(stream_key, shape, pieces, -0.22, 0.18) if pieces else 1.0
    result = jax.random.normal(stream_key, shape, jnp.float32) * width * gain
    return jnp.minimum(jnp.maximum(result, -most), most).astype(held_as)


def setup_inputs(seed: int = 0) -> dict:
    seeds = jax.random.split(jax.random.key(seed), 10)
    return {
        "tokens": scatter_about(seeds[0], (TOKENS, D), 1.0, 6.0, ((0, 16), (1, 16))),
        "init_noise": jnp.clip(jax.random.uniform(seeds[1], (TOKENS, D), jnp.float32, -1.0, 1.0) * shard_levels(seeds[1], (TOKENS, D), ((0, 16), (1, 16)), -0.4, 0.0), -1.0, 1.0),
        "segment_ids": jnp.searchsorted(jnp.cumsum(uneven(seeds[2], EXAMPLES, TOKENS, MOST, 1)), jnp.arange(TOKENS), side="right").astype(jnp.int32),
        "target": scatter_about(seeds[3], (TOKENS, D), 1.0, 6.0, ((0, 16), (1, 16)), jnp.float32),
        "norm_gain": jnp.clip(1.0 + 0.18 * jax.random.normal(seeds[4], (D,), jnp.float32), 0.1, 1.9),
        "weight_in": scatter_about(seeds[5], (D, FF), D ** -0.5, 0.1875, ((1, 16),)),
        "weight_out": scatter_about(seeds[6], (FF, D), FF ** -0.5, 0.03125, ((0, 16),)),
        "moment_in": scatter_about(seeds[7], (D, FF), 0.1, 1.5, ((0, 16), (1, 16)), jnp.float32),
        "moment_out": scatter_about(seeds[8], (FF, D), 0.1, 1.5, ((0, 16), (1, 16)), jnp.float32),
    }


coeff = 0.7978845608
adv_init = 0.5
adv_step = 0.5
decay = 0.9
learn_rate = 0.01

def gelu_value(values):
    tangent = jnp.tanh(coeff * (values + 0.044715 * values * values * values))
    return 0.5 * values * (1.0 + tangent)

def gelu_slope(values):
    tangent = jnp.tanh(coeff * (values + 0.044715 * values * values * values))
    return 0.5 * (1.0 + tangent) + 0.5 * values * (1.0 - tangent * tangent) * coeff * (1.0 + 3.0 * 0.044715 * values * values)

def reference(tokens, init_noise, segment_ids, target, norm_gain, weight_in, weight_out, moment_in, moment_out):
    block = FF // N_TENSOR
    loss_scale = 1.0 / math.sqrt(TOKENS)
    weights_in = weight_in.reshape(D, N_TENSOR, block).transpose(1, 0, 2)
    weights_out = weight_out.reshape(N_TENSOR, block, D)
    labels = jnp.arange(EXAMPLES, dtype=jnp.int32)
    onehot = (segment_ids[:, None] == labels[None, :]).astype(jnp.float32)
    counts = lax.optimization_barrier(jnp.sum(onehot, axis=0))
    perturb = adv_init * init_noise
    grads_in = jnp.zeros((D, FF), jnp.float32)
    grads_out = jnp.zeros((FF, D), jnp.float32)
    for ascent in range(ASCENTS):
        embedded = tokens.astype(jnp.float32) + perturb
        emb_bf = lax.optimization_barrier(embedded.astype(jnp.bfloat16))
        emb_float = emb_bf.astype(jnp.float32)
        inv_rms = lax.rsqrt(lax.optimization_barrier(jnp.mean(emb_float * emb_float, axis=1, keepdims=True)) + 1e-06)
        normed = (emb_float * inv_rms * norm_gain).astype(jnp.bfloat16)

        def forward(running, weights):
            preact = jnp.dot(normed, weights[0], preferred_element_type=jnp.float32)
            hidden = gelu_value(preact).astype(jnp.bfloat16)
            return (running + jnp.dot(hidden, weights[1], preferred_element_type=jnp.float32), None)
        mixed, _ = lax.scan(forward, jnp.zeros((TOKENS, D), jnp.float32), (weights_in, weights_out))
        out_grad = (embedded + mixed - target) * loss_scale
        grad_bf = out_grad.astype(jnp.bfloat16)

        def backward(running, weights):
            preact = jnp.dot(normed, weights[0], preferred_element_type=jnp.float32)
            hidden = gelu_value(preact).astype(jnp.bfloat16)
            hidden_grad = (jnp.dot(grad_bf, weights[1].T, preferred_element_type=jnp.float32) * gelu_slope(preact)).astype(jnp.bfloat16)
            part_in = jnp.dot(normed.T, hidden_grad, preferred_element_type=jnp.float32)
            part_out = jnp.dot(hidden.T, grad_bf, preferred_element_type=jnp.float32)
            running = running + jnp.dot(hidden_grad, weights[0].T, preferred_element_type=jnp.float32)
            return (running, (part_in, part_out))
        normed_grad, (parts_in, parts_out) = lax.scan(backward, jnp.zeros((TOKENS, D), jnp.float32), (weights_in, weights_out))
        grads_in = grads_in + parts_in.transpose(1, 0, 2).reshape(D, FF)
        grads_out = grads_out + parts_out.reshape(FF, D)
        if ascent + 1 < ASCENTS:
            scaled = normed_grad * norm_gain
            row_dot = lax.optimization_barrier(jnp.sum(scaled * emb_float, axis=1, keepdims=True))
            delta_grad = out_grad + inv_rms * scaled - emb_float * inv_rms * inv_rms * inv_rms * row_dot / D
            row_squares = lax.optimization_barrier(jnp.sum(delta_grad * delta_grad, axis=1))
            square_sums = lax.optimization_barrier(jnp.sum(onehot * row_squares[:, None], axis=0))
            root_mean = jnp.sqrt(square_sums / (counts * D) + 1e-06)
            token_scale = lax.optimization_barrier(jnp.sum(onehot * (adv_step / root_mean)[None, :], axis=1))
            perturb = perturb + delta_grad * token_scale[:, None]
    new_moment_in = decay * moment_in + grads_in / ASCENTS
    new_moment_out = decay * moment_out + grads_out / ASCENTS
    new_weight_in = (weight_in.astype(jnp.float32) - learn_rate * new_moment_in).astype(jnp.bfloat16)
    new_weight_out = (weight_out.astype(jnp.float32) - learn_rate * new_moment_out).astype(jnp.bfloat16)
    return (new_weight_in, new_weight_out, new_moment_in, new_moment_out, perturb)
```

```python
import jax
import jax.numpy as jnp
from jax import lax
from jax.sharding import Mesh
from jax.sharding import PartitionSpec as P

D = 1024
ASCENTS = 2
EXAMPLES = 32
DP = ("z_hi", "y", "core")
BLOCKS = ("z_hi", "y")
TENSOR = ("x", "z_lo")

coeff = 0.7978845608
adv_init = 0.5
adv_step = 0.5
decay = 0.9
learn_rate = 0.01


def to_peers(blocks, axis):
    return lax.all_to_all(blocks, axis, 0, 0, tiled=True)


def gathered_features(array):
    copies = jnp.broadcast_to(array, (lax.axis_size(TENSOR), *array.shape))
    blocks = to_peers(copies, TENSOR)
    return jnp.moveaxis(blocks, 0, 1).reshape(array.shape[0], -1)


def feature_blocks(array):
    return jnp.moveaxis(array.reshape(array.shape[0], lax.axis_size(TENSOR), -1), 1, 0)


def from_partner(array, axis):
    return lax.ppermute(array, axis, [(0, 1), (1, 0)])


def gelu_value(values):
    tangent = jnp.tanh(coeff * (values + 0.044715 * values * values * values))
    return 0.5 * values * (1.0 + tangent)


def gelu_slope(values):
    tangent = jnp.tanh(coeff * (values + 0.044715 * values * values * values))
    return 0.5 * (1.0 + tangent) + 0.5 * values * (1.0 - tangent * tangent) * coeff * (
        1.0 + 3.0 * 0.044715 * values * values
    )


def over_neighbours(sums):
    count = lax.axis_size(BLOCKS)
    sums = sums + from_partner(sums, "core")
    before = lax.ppermute(sums, BLOCKS, [(i, i + 1) for i in range(count - 1)])
    after = lax.ppermute(sums, BLOCKS, [(i + 1, i) for i in range(count - 1)])
    return sums + before + after


def halves(array, core):
    width = array.shape[1] // 2
    own = lax.dynamic_slice_in_dim(array, core * width, width, 1)
    other = lax.dynamic_slice_in_dim(array, (1 - core) * width, width, 1)
    return own, other


def summed_over_dp(left, right):
    core, z_hi = lax.axis_index("core"), lax.axis_index("z_hi")
    n_z, n_y = lax.axis_size("z_hi"), lax.axis_size("y")
    half = right.shape[1]
    partial = lax.dot_general(
        left, right, (((0,), (0,)), ((), ())), preferred_element_type=jnp.float32
    ).astype(jnp.bfloat16)
    blocks = jnp.moveaxis(partial.reshape(n_z, n_y, -1, half), 1, 0)
    blocks = to_peers(blocks, "y").astype(jnp.float32)
    sums = jnp.sum(blocks, axis=0)
    own = lax.dynamic_index_in_dim(sums, z_hi, 0, keepdims=False)
    other = lax.dynamic_index_in_dim(sums, 1 - z_hi, 0, keepdims=False)
    rows = own + from_partner(other.astype(jnp.bfloat16), "z_hi").astype(jnp.float32)
    few = rows.shape[0] // 2
    mine = lax.dynamic_slice_in_dim(rows, core * few, few, 0)
    theirs = from_partner(lax.dynamic_slice_in_dim(rows, (1 - core) * few, few, 0), "core")
    return jnp.where(
        core == 0, jnp.concatenate([mine, theirs], 1), jnp.concatenate([theirs, mine], 1)
    )


def shards(
    tokens, init_noise, segment_ids, target, norm_gain, weight_in, weight_out, moment_in, moment_out
):
    dp_count = lax.axis_size(DP)
    local_tokens, width_local = tokens.shape
    loss_scale = (local_tokens * dp_count) ** (-0.5)
    column = lax.axis_index(TENSOR)
    core = lax.axis_index("core")
    gain_local = lax.dynamic_slice_in_dim(norm_gain, column * width_local, width_local)
    labels = jnp.arange(EXAMPLES, dtype=jnp.int32)
    onehot = (segment_ids[:, None] == labels[None, :]).astype(jnp.float32)
    perturb = adv_init * init_noise
    embedded = tokens.astype(jnp.float32) + perturb
    whole = gathered_features(embedded)
    lefts_in, rights_in, lefts_out, rights_out = [], [], [], []
    for ascent in range(ASCENTS):
        emb = lax.optimization_barrier(whole.astype(jnp.bfloat16)).astype(jnp.float32)
        inv_rms = lax.rsqrt(jnp.mean(emb * emb, axis=1, keepdims=True) + 1e-06)
        normed = (emb * inv_rms * norm_gain).astype(jnp.bfloat16)
        preact = jnp.dot(normed, weight_in, preferred_element_type=jnp.float32)
        hidden = gelu_value(preact).astype(jnp.bfloat16)
        partial_value = jnp.dot(hidden, weight_out, preferred_element_type=jnp.float32)
        mixed = jnp.sum(to_peers(feature_blocks(partial_value), TENSOR), axis=0)
        out_grad = (embedded + mixed - target) * loss_scale
        grad_whole = gathered_features(out_grad.astype(jnp.bfloat16))
        hidden_grad = (
            jnp.dot(grad_whole, weight_out.T, preferred_element_type=jnp.float32)
            * gelu_slope(preact)
        ).astype(jnp.bfloat16)
        hidden_own, hidden_other = halves(hidden, core)
        slope_own, slope_other = halves(hidden_grad, core)
        lefts_in += [normed, from_partner(normed, "core")]
        rights_in += [slope_own, from_partner(slope_other, "core")]
        lefts_out += [grad_whole, from_partner(grad_whole, "core")]
        rights_out += [hidden_own, from_partner(hidden_other, "core")]
        if ascent + 1 < ASCENTS:
            normed_partial = jnp.dot(hidden_grad, weight_in.T, preferred_element_type=jnp.float32)
            dot_partial = jnp.sum(normed_partial * norm_gain * emb, axis=1)
            blocks = jnp.concatenate(
                [
                    feature_blocks(normed_partial),
                    jnp.broadcast_to(
                        dot_partial[None, :, None], (lax.axis_size(TENSOR), local_tokens, 1)
                    ),
                ],
                axis=2,
            )
            arrived = jnp.sum(to_peers(blocks, TENSOR), axis=0)
            scaled = arrived[:, :width_local] * gain_local
            row_dot = arrived[:, width_local:]
            emb_local = embedded.astype(jnp.bfloat16).astype(jnp.float32)
            delta_grad = (
                out_grad + inv_rms * scaled - emb_local * inv_rms * inv_rms * inv_rms * row_dot / D
            )
            delta_whole = gathered_features(delta_grad)
            row_squares = jnp.sum(delta_whole * delta_whole, axis=1)
            sums = jnp.stack(
                [jnp.sum(onehot * row_squares[:, None], axis=0), jnp.sum(onehot, axis=0)]
            )
            square_sums, counts = over_neighbours(sums)
            root_mean = jnp.sqrt(square_sums / (jnp.maximum(counts, 1.0) * D) + 1e-06)
            token_scale = jnp.sum(onehot * (adv_step / root_mean)[None, :], axis=1)[:, None]
            perturb = perturb + delta_grad * token_scale
            embedded = tokens.astype(jnp.float32) + perturb
            whole = whole + delta_whole * token_scale
    summed_out = summed_over_dp(
        jnp.concatenate(lefts_out, 0), jnp.concatenate(rights_out, 0)
    ).T
    summed_in = summed_over_dp(jnp.concatenate(lefts_in, 0), jnp.concatenate(rights_in, 0))
    dp_rows = moment_in.shape[0]
    offset = lax.axis_index(DP) * dp_rows
    own_in = lax.dynamic_slice_in_dim(weight_in, offset, dp_rows, 0)
    own_out = lax.dynamic_slice_in_dim(weight_out, offset, dp_rows, 1)
    new_moment_in = decay * moment_in + summed_in / ASCENTS
    new_moment_out = decay * moment_out + summed_out / ASCENTS
    new_weight_in = (own_in.astype(jnp.float32) - learn_rate * new_moment_in).astype(jnp.bfloat16)
    new_weight_out = (own_out.astype(jnp.float32) - learn_rate * new_moment_out).astype(
        jnp.bfloat16
    )
    return (new_weight_in, new_weight_out, new_moment_in, new_moment_out, perturb)


def solution(mesh):
    torus = Mesh(mesh.devices.reshape(2, 4, 2, 4, 4), DP + TENSOR)
    in_specs = (
        P(DP, TENSOR),
        P(DP, TENSOR),
        P(DP),
        P(DP, TENSOR),
        P(),
        P(None, TENSOR),
        P(TENSOR, None),
        P(DP, TENSOR),
        P(TENSOR, DP),
    )
    out_specs = (P(DP, TENSOR), P(TENSOR, DP), P(DP, TENSOR), P(TENSOR, DP), P(DP, TENSOR))
    return jax.shard_map(
        shards, mesh=torus, in_specs=in_specs, out_specs=out_specs, check_vma=False
    )
```

```python
import jax
import jax.numpy as jnp
from jax import lax
from jax.sharding import Mesh
from jax.sharding import PartitionSpec as P

D = 1024
ASCENTS = 2
EXAMPLES = 32
DP = ("z_hi", "y", "core")
BLOCKS = ("z_hi", "y")
TENSOR = ("x", "z_lo")

coeff = 0.7978845608
adv_init = 0.5
adv_step = 0.5
decay = 0.9
learn_rate = 0.01


def to_peers(blocks, axis):
    return lax.all_to_all(blocks, axis, 0, 0, tiled=True)


def gathered_features(array):
    copies = jnp.broadcast_to(array, (lax.axis_size(TENSOR), *array.shape))
    blocks = to_peers(copies, TENSOR)
    return jnp.moveaxis(blocks, 0, 1).reshape(array.shape[0], -1)


def gathered_for_both(array):
    axes = ("z_hi", *TENSOR)
    copies = jnp.broadcast_to(array, (lax.axis_size(axes), *array.shape))
    blocks = to_peers(copies, axes).reshape(2, -1, *array.shape)
    z_hi = lax.axis_index("z_hi")

    def whole(index):
        some = lax.dynamic_index_in_dim(blocks, index, 0, keepdims=False)
        return jnp.moveaxis(some, 0, 1).reshape(array.shape[0], -1)

    return whole(z_hi), whole(1 - z_hi)


def feature_blocks(array):
    return jnp.moveaxis(array.reshape(array.shape[0], lax.axis_size(TENSOR), -1), 1, 0)


def over_tensor(blocks):
    return jnp.sum(to_peers(blocks, TENSOR).astype(jnp.float32), axis=0)


def from_partner(array, axis):
    return lax.ppermute(array, axis, [(0, 1), (1, 0)])


def gelu_and_slope(values):
    tangent = jnp.tanh(coeff * (values + 0.044715 * values * values * values))
    value = 0.5 * values * (1.0 + tangent)
    slope = 0.5 * (1.0 + tangent) + 0.5 * values * (1.0 - tangent * tangent) * coeff * (
        1.0 + 3.0 * 0.044715 * values * values
    )
    return lax.optimization_barrier((value.astype(jnp.bfloat16), slope))


def over_neighbours(sums):
    count = lax.axis_size(BLOCKS)
    sums = sums + from_partner(sums, "core")
    before = lax.ppermute(sums, BLOCKS, [(i, i + 1) for i in range(count - 1)])
    after = lax.ppermute(sums, BLOCKS, [(i + 1, i) for i in range(count - 1)])
    return sums + before + after


def half_of(array, index, dim):
    width = array.shape[dim] // 2
    return lax.dynamic_slice_in_dim(array, index * width, width, dim)


def summed_over_dp(left, right):
    core, y = lax.axis_index("core"), lax.axis_index("y")
    n_y = lax.axis_size("y")
    partial = lax.dot_general(
        left, right, (((0,), (0,)), ((), ())), preferred_element_type=jnp.float32
    ).astype(jnp.bfloat16)
    blocks = partial.reshape(n_y, -1, right.shape[1])
    rows = lax.dynamic_index_in_dim(blocks, y, 0, keepdims=False).astype(jnp.float32)
    for shift in range(1, n_y):
        sent = lax.dynamic_index_in_dim(blocks, lax.rem(y + shift, n_y), 0, keepdims=False)
        ring = [(i, (i + shift) % n_y) for i in range(n_y)]
        rows = rows + lax.ppermute(sent, "y", ring).astype(jnp.float32)
    mine = half_of(rows, core, 0)
    theirs = from_partner(half_of(rows, 1 - core, 0), "core")
    return jnp.where(
        core == 0, jnp.concatenate([mine, theirs], 1), jnp.concatenate([theirs, mine], 1)
    )


def shards(
    tokens, init_noise, segment_ids, target, norm_gain, weight_in, weight_out, moment_in, moment_out
):
    dp_count = lax.axis_size(DP)
    local_tokens, width_local = tokens.shape
    loss_scale = (local_tokens * dp_count) ** (-0.5)
    column = lax.axis_index(TENSOR)
    core, z_hi = lax.axis_index("core"), lax.axis_index("z_hi")
    gain_local = lax.dynamic_slice_in_dim(norm_gain, column * width_local, width_local)
    labels = jnp.arange(EXAMPLES, dtype=jnp.int32)
    onehot = (segment_ids[:, None] == labels[None, :]).astype(jnp.float32)
    perturb = adv_init * init_noise
    embedded = tokens.astype(jnp.float32) + perturb
    whole = gathered_features(embedded)
    half_in, half_out = half_of(weight_in, core, 1), half_of(weight_out, core, 0)
    lefts_in, rights_in, lefts_out, rights_out = [], [], [], []
    for ascent in range(ASCENTS):
        last = ascent + 1 == ASCENTS
        emb = lax.optimization_barrier(whole.astype(jnp.bfloat16)).astype(jnp.float32)
        inv_rms = lax.rsqrt(jnp.mean(emb * emb, axis=1, keepdims=True) + 1e-06)
        normed = (emb * inv_rms * norm_gain).astype(jnp.bfloat16)
        preact = jnp.dot(normed, weight_in, preferred_element_type=jnp.float32)
        hidden, slope = gelu_and_slope(preact)
        partial_value = jnp.dot(hidden, weight_out, preferred_element_type=jnp.float32)
        mixed = over_tensor(feature_blocks(partial_value.astype(jnp.bfloat16)))
        far_normed = from_partner(normed, "z_hi")
        far_normed = jnp.concatenate([far_normed, from_partner(far_normed, "core")], 0)
        far_preact = jnp.dot(far_normed, half_in, preferred_element_type=jnp.float32)
        far_hidden, far_slope = gelu_and_slope(far_preact)
        near_hidden = [half_of(hidden, core, 1), from_partner(half_of(hidden, 1 - core, 1), "core")]
        rights_out += [*near_hidden, far_hidden]
        some_normed = half_of(normed, z_hi, 1)
        lefts_in += [some_normed, from_partner(some_normed, "core"), half_of(far_normed, z_hi, 1)]
        out_grad = (embedded + mixed - target) * loss_scale
        if last:
            grad, far_grad = gathered_for_both(out_grad.astype(jnp.bfloat16))
        else:
            grad = gathered_features(out_grad.astype(jnp.bfloat16))
            far_grad = from_partner(grad, "z_hi")
        some_grad = half_of(grad, z_hi, 1)
        far_grad = jnp.concatenate([far_grad, from_partner(far_grad, "core")], 0)
        lefts_out += [some_grad, from_partner(some_grad, "core"), half_of(far_grad, z_hi, 1)]
        hidden_grad = (
            jnp.dot(grad, weight_out.T, preferred_element_type=jnp.float32) * slope
        ).astype(jnp.bfloat16)
        far_hidden_grad = (
            jnp.dot(far_grad, half_out.T, preferred_element_type=jnp.float32) * far_slope
        ).astype(jnp.bfloat16)
        rights_in += [
            half_of(hidden_grad, core, 1),
            from_partner(half_of(hidden_grad, 1 - core, 1), "core"),
            far_hidden_grad,
        ]
        if not last:
            normed_partial = jnp.dot(hidden_grad, weight_in.T, preferred_element_type=jnp.float32)
            dot_partial = jnp.sum(normed_partial * norm_gain * emb, axis=1)
            dot_head = dot_partial.astype(jnp.bfloat16)
            dot_rest = (dot_partial - dot_head.astype(jnp.float32)).astype(jnp.bfloat16)
            dots = jnp.stack([dot_head, dot_rest], 1)[None]
            blocks = jnp.concatenate(
                [
                    feature_blocks(normed_partial.astype(jnp.bfloat16)),
                    jnp.broadcast_to(dots, (lax.axis_size(TENSOR), local_tokens, 2)),
                ],
                axis=2,
            )
            arrived = over_tensor(blocks)
            scaled = arrived[:, :width_local] * gain_local
            row_dot = jnp.sum(arrived[:, width_local:], axis=1, keepdims=True)
            emb_local = embedded.astype(jnp.bfloat16).astype(jnp.float32)
            delta_grad = (
                out_grad + inv_rms * scaled - emb_local * inv_rms * inv_rms * inv_rms * row_dot / D
            )
            delta_whole = gathered_features(delta_grad.astype(jnp.bfloat16)).astype(jnp.float32)
            row_squares = jnp.sum(delta_whole * delta_whole, axis=1)
            sums = jnp.stack(
                [jnp.sum(onehot * row_squares[:, None], axis=0), jnp.sum(onehot, axis=0)]
            )
            square_sums, counts = over_neighbours(sums)
            root_mean = jnp.sqrt(square_sums / (jnp.maximum(counts, 1.0) * D) + 1e-06)
            token_scale = jnp.sum(onehot * (adv_step / root_mean)[None, :], axis=1)[:, None]
            perturb = perturb + delta_grad * token_scale
            embedded = tokens.astype(jnp.float32) + perturb
            whole = whole + delta_whole * token_scale
    summed_out = summed_over_dp(
        jnp.concatenate(lefts_out, 0), jnp.concatenate(rights_out, 0)
    ).T
    summed_in = summed_over_dp(jnp.concatenate(lefts_in, 0), jnp.concatenate(rights_in, 0))
    dp_rows = moment_in.shape[0]
    offset = lax.axis_index(DP) * dp_rows
    own_in = lax.dynamic_slice_in_dim(weight_in, offset, dp_rows, 0)
    own_out = lax.dynamic_slice_in_dim(weight_out, offset, dp_rows, 1)
    new_moment_in = decay * moment_in + summed_in / ASCENTS
    new_moment_out = decay * moment_out + summed_out / ASCENTS
    new_weight_in = (own_in.astype(jnp.float32) - learn_rate * new_moment_in).astype(jnp.bfloat16)
    new_weight_out = (own_out.astype(jnp.float32) - learn_rate * new_moment_out).astype(
        jnp.bfloat16
    )
    return (new_weight_in, new_weight_out, new_moment_in, new_moment_out, perturb)


def solution(mesh):
    torus = Mesh(mesh.devices.reshape(2, 4, 2, 4, 4), DP + TENSOR)
    in_specs = (
        P(DP, TENSOR),
        P(DP, TENSOR),
        P(DP),
        P(DP, TENSOR),
        P(),
        P(None, TENSOR),
        P(TENSOR, None),
        P(DP, TENSOR),
        P(TENSOR, DP),
    )
    out_specs = (P(DP, TENSOR), P(TENSOR, DP), P(DP, TENSOR), P(TENSOR, DP), P(DP, TENSOR))
    return jax.shard_map(
        shards, mesh=torus, in_specs=in_specs, out_specs=out_specs, check_vma=False
    )
```

```python
import jax
import jax.numpy as jnp
from jax import lax
from jax.sharding import Mesh
from jax.sharding import PartitionSpec as P

D = 1024
ASCENTS = 2
EXAMPLES = 32
DP = ("z_hi", "y", "core")
BLOCKS = ("z_hi", "y")
TENSOR = ("x", "z_lo")

coeff = 0.7978845608
adv_init = 0.5
adv_step = 0.5
decay = 0.9
learn_rate = 0.01


def to_peers(blocks, axis):
    return lax.all_to_all(blocks, axis, 0, 0, tiled=True)


def gathered_features(array):
    copies = jnp.broadcast_to(array, (lax.axis_size(TENSOR), *array.shape))
    blocks = to_peers(copies, TENSOR)
    return jnp.moveaxis(blocks, 0, 1).reshape(array.shape[0], -1)


def feature_blocks(array):
    return jnp.moveaxis(array.reshape(array.shape[0], lax.axis_size(TENSOR), -1), 1, 0)


def over_tensor(blocks):
    return jnp.sum(to_peers(blocks, TENSOR).astype(jnp.float32), axis=0)


def from_partner(array, axis):
    return lax.ppermute(array, axis, [(0, 1), (1, 0)])


def gelu_and_slope(values):
    tangent = jnp.tanh(coeff * (values + 0.044715 * values * values * values))
    value = 0.5 * values * (1.0 + tangent)
    slope = 0.5 * (1.0 + tangent) + 0.5 * values * (1.0 - tangent * tangent) * coeff * (
        1.0 + 3.0 * 0.044715 * values * values
    )
    return lax.optimization_barrier((value.astype(jnp.bfloat16), slope))


def over_neighbours(sums):
    count = lax.axis_size(BLOCKS)
    sums = sums + from_partner(sums, "core")
    before = lax.ppermute(sums, BLOCKS, [(i, i + 1) for i in range(count - 1)])
    after = lax.ppermute(sums, BLOCKS, [(i + 1, i) for i in range(count - 1)])
    return sums + before + after


def rows_of_core(array, core):
    tokens, features = array.shape
    blocks = array.reshape(tokens, lax.axis_size(BLOCKS), 2, -1)
    return lax.dynamic_index_in_dim(blocks, core, 2, keepdims=False).reshape(tokens, features // 2)


def for_both_cores(array, core):
    return [rows_of_core(array, core), from_partner(rows_of_core(array, 1 - core), "core")]


def picked(blocks, index, dim):
    return lax.dynamic_index_in_dim(blocks, index, dim, keepdims=False)


def over_y(blocks, dim):
    y, n_y = lax.axis_index("y"), lax.axis_size("y")
    total = picked(blocks, y, dim).astype(jnp.float32)
    for shift in range(1, n_y):
        ring = [(i, (i + shift) % n_y) for i in range(n_y)]
        sent = picked(blocks, lax.rem(y + shift, n_y), dim).astype(jnp.bfloat16)
        total = total + lax.ppermute(sent, "y", ring).astype(jnp.float32)
    return total


def over_z(blocks):
    z_hi = lax.axis_index("z_hi")
    sent = picked(blocks, 1 - z_hi, 0).astype(jnp.bfloat16)
    return picked(blocks, z_hi, 0).astype(jnp.float32) + from_partner(sent, "z_hi").astype(
        jnp.float32
    )


def summed_over_dp(lefts, rights):
    left, right = jnp.concatenate(lefts, 0), jnp.concatenate(rights, 0)
    partial = lax.dot_general(
        left, right, (((0,), (0,)), ((), ())), preferred_element_type=jnp.float32
    ).astype(jnp.bfloat16)
    blocks = partial.reshape(lax.axis_size("z_hi"), lax.axis_size("y"), -1, right.shape[1])
    return over_z(over_y(blocks, 1))


def shards(
    tokens, init_noise, segment_ids, target, norm_gain, weight_in, weight_out, moment_in, moment_out
):
    dp_count = lax.axis_size(DP)
    local_tokens, width_local = tokens.shape
    loss_scale = (local_tokens * dp_count) ** (-0.5)
    column = lax.axis_index(TENSOR)
    core = lax.axis_index("core")
    gain_local = lax.dynamic_slice_in_dim(norm_gain, column * width_local, width_local)
    labels = jnp.arange(EXAMPLES, dtype=jnp.int32)
    onehot = (segment_ids[:, None] == labels[None, :]).astype(jnp.float32)
    perturb = adv_init * init_noise
    embedded = tokens.astype(jnp.float32) + perturb
    whole = gathered_features(embedded)
    lefts_in, rights_in, lefts_out, rights_out = [], [], [], []
    for ascent in range(ASCENTS):
        last = ascent + 1 == ASCENTS
        emb = lax.optimization_barrier(whole.astype(jnp.bfloat16)).astype(jnp.float32)
        inv_rms = lax.rsqrt(jnp.mean(emb * emb, axis=1, keepdims=True) + 1e-06)
        normed = (emb * inv_rms * norm_gain).astype(jnp.bfloat16)
        preact = jnp.dot(normed, weight_in, preferred_element_type=jnp.float32)
        hidden, slope = gelu_and_slope(preact)
        partial_value = jnp.dot(hidden, weight_out, preferred_element_type=jnp.float32)
        mixed = over_tensor(feature_blocks(partial_value.astype(jnp.bfloat16)))
        rights_out += [hidden, from_partner(hidden, "core")]
        lefts_in += for_both_cores(normed, core)
        out_grad = (embedded + mixed - target) * loss_scale
        grad = gathered_features(out_grad.astype(jnp.bfloat16))
        lefts_out += for_both_cores(grad, core)
        if last:
            summed_out = summed_over_dp(lefts_out, rights_out).T
        hidden_grad = (
            jnp.dot(grad, weight_out.T, preferred_element_type=jnp.float32) * slope
        ).astype(jnp.bfloat16)
        rights_in += [hidden_grad, from_partner(hidden_grad, "core")]
        if not last:
            normed_partial = jnp.dot(hidden_grad, weight_in.T, preferred_element_type=jnp.float32)
            dot_partial = jnp.sum(normed_partial * norm_gain * emb, axis=1)
            dot_head = dot_partial.astype(jnp.bfloat16)
            dot_rest = (dot_partial - dot_head.astype(jnp.float32)).astype(jnp.bfloat16)
            dots = jnp.stack([dot_head, dot_rest], 1)[None]
            blocks = jnp.concatenate(
                [
                    feature_blocks(normed_partial.astype(jnp.bfloat16)),
                    jnp.broadcast_to(dots, (lax.axis_size(TENSOR), local_tokens, 2)),
                ],
                axis=2,
            )
            arrived = over_tensor(blocks)
            scaled = arrived[:, :width_local] * gain_local
            row_dot = jnp.sum(arrived[:, width_local:], axis=1, keepdims=True)
            emb_local = embedded.astype(jnp.bfloat16).astype(jnp.float32)
            delta_grad = (
                out_grad + inv_rms * scaled - emb_local * inv_rms * inv_rms * inv_rms * row_dot / D
            )
            delta_whole = gathered_features(delta_grad.astype(jnp.bfloat16)).astype(jnp.float32)
            row_squares = jnp.sum(delta_whole * delta_whole, axis=1)
            sums = jnp.stack(
                [jnp.sum(onehot * row_squares[:, None], axis=0), jnp.sum(onehot, axis=0)]
            )
            square_sums, counts = over_neighbours(sums)
            root_mean = jnp.sqrt(square_sums / (jnp.maximum(counts, 1.0) * D) + 1e-06)
            token_scale = jnp.sum(onehot * (adv_step / root_mean)[None, :], axis=1)[:, None]
            perturb = perturb + delta_grad * token_scale
            embedded = tokens.astype(jnp.float32) + perturb
            whole = whole + delta_whole * token_scale
    summed_in = summed_over_dp(lefts_in, rights_in)
    dp_rows = moment_in.shape[0]
    offset = lax.axis_index(DP) * dp_rows
    own_in = lax.dynamic_slice_in_dim(weight_in, offset, dp_rows, 0)
    own_out = lax.dynamic_slice_in_dim(weight_out, offset, dp_rows, 1)
    new_moment_in = decay * moment_in + summed_in / ASCENTS
    new_moment_out = decay * moment_out + summed_out / ASCENTS
    new_weight_in = (own_in.astype(jnp.float32) - learn_rate * new_moment_in).astype(jnp.bfloat16)
    new_weight_out = (own_out.astype(jnp.float32) - learn_rate * new_moment_out).astype(
        jnp.bfloat16
    )
    return (new_weight_in, new_weight_out, new_moment_in, new_moment_out, perturb)


def solution(mesh):
    torus = Mesh(mesh.devices.reshape(2, 4, 2, 4, 4), DP + TENSOR)
    in_specs = (
        P(DP, TENSOR),
        P(DP, TENSOR),
        P(DP),
        P(DP, TENSOR),
        P(),
        P(None, TENSOR),
        P(TENSOR, None),
        P(DP, TENSOR),
        P(TENSOR, DP),
    )
    out_specs = (P(DP, TENSOR), P(TENSOR, DP), P(DP, TENSOR), P(TENSOR, DP), P(DP, TENSOR))
    return jax.shard_map(
        shards, mesh=torus, in_specs=in_specs, out_specs=out_specs, check_vma=False
    )
```

```python
import jax
import jax.numpy as jnp
from jax import lax
from jax.sharding import Mesh
from jax.sharding import PartitionSpec as P

D = 1024
ASCENTS = 2
EXAMPLES = 32
DP = ("z_hi", "y", "core")
BLOCKS = ("z_hi", "y")
TENSOR = ("x", "z_lo")

coeff = 0.7978845608
adv_init = 0.5
adv_step = 0.5
decay = 0.9
learn_rate = 0.01


def to_peers(blocks, axis):
    return lax.all_to_all(blocks, axis, 0, 0, tiled=True)


def gathered_features(array):
    copies = jnp.broadcast_to(array, (lax.axis_size(TENSOR), *array.shape))
    blocks = to_peers(copies, TENSOR)
    return jnp.moveaxis(blocks, 0, 1).reshape(array.shape[0], -1)


def feature_blocks(array):
    return jnp.moveaxis(array.reshape(array.shape[0], lax.axis_size(TENSOR), -1), 1, 0)


def over_tensor(blocks):
    return jnp.sum(to_peers(blocks, TENSOR).astype(jnp.float32), axis=0)


def from_partner(array, axis):
    return lax.ppermute(array, axis, [(0, 1), (1, 0)])


def gelu_and_slope(values):
    tangent = jnp.tanh(coeff * (values + 0.044715 * values * values * values))
    value = 0.5 * values * (1.0 + tangent)
    slope = 0.5 * (1.0 + tangent) + 0.5 * values * (1.0 - tangent * tangent) * coeff * (
        1.0 + 3.0 * 0.044715 * values * values
    )
    return lax.optimization_barrier((value.astype(jnp.bfloat16), slope))


def over_neighbours(sums):
    count = lax.axis_size(BLOCKS)
    sums = sums + from_partner(sums, "core")
    before = lax.ppermute(sums, BLOCKS, [(i, i + 1) for i in range(count - 1)])
    after = lax.ppermute(sums, BLOCKS, [(i + 1, i) for i in range(count - 1)])
    return sums + before + after


def rows_of_core(array, core):
    tokens, features = array.shape
    blocks = array.reshape(tokens, lax.axis_size(BLOCKS), 2, -1)
    return lax.dynamic_index_in_dim(blocks, core, 2, keepdims=False).reshape(tokens, features // 2)


def for_both_cores(array, core):
    return [rows_of_core(array, core), from_partner(rows_of_core(array, 1 - core), "core")]


def picked(blocks, index, dim):
    return lax.dynamic_index_in_dim(blocks, index, dim, keepdims=False)


def over_y(blocks):
    y, n_y = lax.axis_index("y"), lax.axis_size("y")
    up = [(i, (i + 1) % n_y) for i in range(n_y)]
    down = [(i, (i - 1) % n_y) for i in range(n_y)]
    at = lambda shift: lax.rem(y + shift, n_y)
    across = picked(blocks, at(2), 1)
    from_below = lax.ppermute(across[0], "y", up).astype(jnp.float32)
    from_above = lax.ppermute(across[1], "y", down).astype(jnp.float32)
    above = picked(blocks, at(1), 1).astype(jnp.float32)
    below = picked(blocks, at(n_y - 1), 1).astype(jnp.float32)
    above = jnp.stack([above[0] + from_below, above[1]]).astype(jnp.bfloat16)
    below = jnp.stack([below[0], below[1] + from_above]).astype(jnp.bfloat16)
    above, below = lax.optimization_barrier((above, below))
    arrived = lax.ppermute(above, "y", up).astype(jnp.float32) + lax.ppermute(
        below, "y", down
    ).astype(jnp.float32)
    return picked(blocks, y, 1).astype(jnp.float32) + arrived


def nothing(value):
    return jnp.minimum(jnp.abs(value.astype(jnp.float32)), 0.0)


def over_z(blocks, earlier):
    z_hi = lax.axis_index("z_hi")
    sent = (picked(blocks, 1 - z_hi, 0) + nothing(earlier)).astype(jnp.bfloat16)
    total = picked(blocks, z_hi, 0) + from_partner(sent, "z_hi").astype(jnp.float32)
    return total


def partial_over_chip(lefts, rights):
    left, right = jnp.concatenate(lefts, 0), jnp.concatenate(rights, 0)
    return lax.dot_general(
        left, right, (((0,), (0,)), ((), ())), preferred_element_type=jnp.float32
    ).astype(jnp.bfloat16)


def summed_over_dp(partial, earlier):
    blocks = partial.reshape(lax.axis_size("z_hi"), lax.axis_size("y"), -1, partial.shape[1])
    return over_z(over_y(blocks), earlier)


def shards(
    tokens, init_noise, segment_ids, target, norm_gain, weight_in, weight_out, moment_in, moment_out
):
    dp_count = lax.axis_size(DP)
    local_tokens, width_local = tokens.shape
    loss_scale = (local_tokens * dp_count) ** (-0.5)
    column = lax.axis_index(TENSOR)
    core = lax.axis_index("core")
    gain_local = lax.dynamic_slice_in_dim(norm_gain, column * width_local, width_local)
    labels = jnp.arange(EXAMPLES, dtype=jnp.int32)
    onehot = (segment_ids[:, None] == labels[None, :]).astype(jnp.float32)
    perturb = adv_init * init_noise
    embedded = tokens.astype(jnp.float32) + perturb
    whole = gathered_features(embedded)
    lefts_in, rights_in, lefts_out, rights_out = [], [], [], []
    for ascent in range(ASCENTS):
        last = ascent + 1 == ASCENTS
        emb = lax.optimization_barrier(whole.astype(jnp.bfloat16)).astype(jnp.float32)
        inv_rms = lax.rsqrt(jnp.mean(emb * emb, axis=1, keepdims=True) + 1e-06)
        normed = (emb * inv_rms * norm_gain).astype(jnp.bfloat16)
        preact = jnp.dot(normed, weight_in, preferred_element_type=jnp.float32)
        hidden, slope = gelu_and_slope(preact)
        partial_value = jnp.dot(hidden, weight_out, preferred_element_type=jnp.float32)
        mixed = over_tensor(feature_blocks(partial_value.astype(jnp.bfloat16)))
        rights_out += [hidden, from_partner(hidden, "core")]
        lefts_in += for_both_cores(normed, core)
        out_grad = (embedded + mixed - target) * loss_scale
        grad = gathered_features(out_grad.astype(jnp.bfloat16))
        lefts_out += for_both_cores(grad, core)
        if last:
            partial_out = partial_over_chip(lefts_out, rights_out)
            summed_out = summed_over_dp(partial_out, partial_out[0, 0])
            slope = slope + nothing(partial_out[0, 0])
        hidden_grad = (
            jnp.dot(grad, weight_out.T, preferred_element_type=jnp.float32) * slope
        ).astype(jnp.bfloat16)
        rights_in += [hidden_grad, from_partner(hidden_grad, "core")]
        if not last:
            normed_partial = jnp.dot(hidden_grad, weight_in.T, preferred_element_type=jnp.float32)
            dot_partial = jnp.sum(normed_partial * norm_gain * emb, axis=1)
            dot_head = dot_partial.astype(jnp.bfloat16)
            dot_rest = (dot_partial - dot_head.astype(jnp.float32)).astype(jnp.bfloat16)
            dots = jnp.stack([dot_head, dot_rest], 1)[None]
            blocks = jnp.concatenate(
                [
                    feature_blocks(normed_partial.astype(jnp.bfloat16)),
                    jnp.broadcast_to(dots, (lax.axis_size(TENSOR), local_tokens, 2)),
                ],
                axis=2,
            )
            arrived = over_tensor(blocks)
            scaled = arrived[:, :width_local] * gain_local
            row_dot = jnp.sum(arrived[:, width_local:], axis=1, keepdims=True)
            emb_local = embedded.astype(jnp.bfloat16).astype(jnp.float32)
            delta_grad = (
                out_grad + inv_rms * scaled - emb_local * inv_rms * inv_rms * inv_rms * row_dot / D
            )
            delta_whole = gathered_features(delta_grad.astype(jnp.bfloat16)).astype(jnp.float32)
            row_squares = jnp.sum(delta_whole * delta_whole, axis=1)
            sums = jnp.stack(
                [jnp.sum(onehot * row_squares[:, None], axis=0), jnp.sum(onehot, axis=0)]
            )
            square_sums, counts = over_neighbours(sums)
            root_mean = jnp.sqrt(square_sums / (jnp.maximum(counts, 1.0) * D) + 1e-06)
            token_scale = jnp.sum(onehot * (adv_step / root_mean)[None, :], axis=1)[:, None]
            perturb = perturb + delta_grad * token_scale
            embedded = tokens.astype(jnp.float32) + perturb
            whole = whole + delta_whole * token_scale
    partial_in = partial_over_chip(lefts_in, rights_in)
    summed_in, summed_out = summed_over_dp(partial_in, summed_out[0, 0]), summed_out.T
    dp_rows = moment_in.shape[0]
    offset = lax.axis_index(DP) * dp_rows
    own_in = lax.dynamic_slice_in_dim(weight_in, offset, dp_rows, 0)
    own_out = lax.dynamic_slice_in_dim(weight_out, offset, dp_rows, 1)
    new_moment_in = decay * moment_in + summed_in / ASCENTS
    new_moment_out = decay * moment_out + summed_out / ASCENTS
    new_weight_in = (own_in.astype(jnp.float32) - learn_rate * new_moment_in).astype(jnp.bfloat16)
    new_weight_out = (own_out.astype(jnp.float32) - learn_rate * new_moment_out).astype(
        jnp.bfloat16
    )
    return (new_weight_in, new_weight_out, new_moment_in, new_moment_out, perturb)


def solution(mesh):
    torus = Mesh(mesh.devices.reshape(2, 4, 2, 4, 4), DP + TENSOR)
    in_specs = (
        P(DP, TENSOR),
        P(DP, TENSOR),
        P(DP),
        P(DP, TENSOR),
        P(),
        P(None, TENSOR),
        P(TENSOR, None),
        P(DP, TENSOR),
        P(TENSOR, DP),
    )
    out_specs = (P(DP, TENSOR), P(TENSOR, DP), P(DP, TENSOR), P(TENSOR, DP), P(DP, TENSOR))
    return jax.shard_map(
        shards, mesh=torus, in_specs=in_specs, out_specs=out_specs, check_vma=False
    )
```

```python
import jax
import jax.numpy as jnp
from jax import lax
from jax.sharding import Mesh
from jax.sharding import PartitionSpec as P

D = 1024
ASCENTS = 2
EXAMPLES = 32
DP = ("z_hi", "y", "core")
BLOCKS = ("z_hi", "y")
TENSOR = ("x", "z_lo")

coeff = 0.7978845608
adv_init = 0.5
adv_step = 0.5
decay = 0.9
learn_rate = 0.01


def to_peers(blocks, axis):
    return lax.all_to_all(blocks, axis, 0, 0, tiled=True)


def gathered_features(array):
    copies = jnp.broadcast_to(array, (lax.axis_size(TENSOR), *array.shape))
    blocks = to_peers(copies, TENSOR)
    return jnp.moveaxis(blocks, 0, 1).reshape(array.shape[0], -1)


def feature_blocks(array):
    return jnp.moveaxis(array.reshape(array.shape[0], lax.axis_size(TENSOR), -1), 1, 0)


def over_tensor(blocks):
    return jnp.sum(to_peers(blocks, TENSOR).astype(jnp.float32), axis=0)


def from_partner(array, axis):
    return lax.ppermute(array, axis, [(0, 1), (1, 0)])


def gelu_and_slope(values):
    tangent = jnp.tanh(coeff * (values + 0.044715 * values * values * values))
    value = 0.5 * values * (1.0 + tangent)
    slope = 0.5 * (1.0 + tangent) + 0.5 * values * (1.0 - tangent * tangent) * coeff * (
        1.0 + 3.0 * 0.044715 * values * values
    )
    return lax.optimization_barrier((value.astype(jnp.bfloat16), slope))


def over_neighbours(sums):
    count = lax.axis_size(BLOCKS)
    sums = sums + from_partner(sums, "core")
    before = lax.ppermute(sums, BLOCKS, [(i, i + 1) for i in range(count - 1)])
    after = lax.ppermute(sums, BLOCKS, [(i + 1, i) for i in range(count - 1)])
    return sums + before + after


def rows_of_core(array, core):
    tokens, features = array.shape
    blocks = array.reshape(tokens, lax.axis_size(BLOCKS), 2, -1)
    return lax.dynamic_index_in_dim(blocks, core, 2, keepdims=False).reshape(tokens, features // 2)


def for_both_cores(array, core):
    return [rows_of_core(array, core), from_partner(rows_of_core(array, 1 - core), "core")]


def picked(blocks, index, dim):
    return lax.dynamic_index_in_dim(blocks, index, dim, keepdims=False)


def over_y(blocks, late):
    y, n_y = lax.axis_index("y"), lax.axis_size("y")
    up = [(i, (i + 1) % n_y) for i in range(n_y)]
    down = [(i, (i - 1) % n_y) for i in range(n_y)]

    def block(z_hi, shift):
        return picked(blocks, z_hi * n_y + lax.rem(y + shift, n_y), 0)

    def with_own(own, arrived):
        return own.astype(jnp.float32) + arrived.astype(jnp.float32)

    risen = lax.ppermute(jnp.stack([block(0, 2), block(1, 1)]), "y", up)
    sunk = lax.ppermute(jnp.stack([block(1, 2), block(0, n_y - 1)]), "y", down)
    on_up = (with_own(block(0, 1), risen[0]) + late).astype(jnp.bfloat16)
    on_down = (with_own(block(1, n_y - 1), sunk[0]) + late).astype(jnp.bfloat16)
    on_up, on_down = lax.optimization_barrier((on_up, on_down))
    first = with_own(with_own(block(0, 0), sunk[1]), lax.ppermute(on_up, "y", up))
    second = with_own(with_own(block(1, 0), risen[1]), lax.ppermute(on_down, "y", down))
    return first, second


def nothing(value):
    return jnp.minimum(jnp.abs(value.astype(jnp.float32)), 0.0)


def over_z(totals, late):
    first, second = totals
    low = lax.axis_index("z_hi") == 0
    sent = (jnp.where(low, second, first) + late).astype(jnp.bfloat16)
    return jnp.where(low, first, second) + from_partner(sent, "z_hi").astype(jnp.float32)


def partial_over_chip(lefts, rights):
    left, right = jnp.concatenate(lefts, 0), jnp.concatenate(rights, 0)
    return lax.dot_general(
        left, right, (((0,), (0,)), ((), ())), preferred_element_type=jnp.float32
    ).astype(jnp.bfloat16)


def summed_over_dp(partial, late_y, late_z):
    blocks = partial.reshape(lax.axis_size(BLOCKS), -1, partial.shape[1])
    return over_z(over_y(blocks, late_y), late_z)


def shards(
    tokens, init_noise, segment_ids, target, norm_gain, weight_in, weight_out, moment_in, moment_out
):
    dp_count = lax.axis_size(DP)
    local_tokens, width_local = tokens.shape
    loss_scale = (local_tokens * dp_count) ** (-0.5)
    column = lax.axis_index(TENSOR)
    core = lax.axis_index("core")
    gain_local = lax.dynamic_slice_in_dim(norm_gain, column * width_local, width_local)
    labels = jnp.arange(EXAMPLES, dtype=jnp.int32)
    onehot = (segment_ids[:, None] == labels[None, :]).astype(jnp.float32)
    perturb = adv_init * init_noise
    embedded = tokens.astype(jnp.float32) + perturb
    emb_local = embedded.astype(jnp.bfloat16)
    emb_bf = gathered_features(emb_local)
    lefts_in, rights_in, lefts_out, rights_out = [], [], [], []
    for ascent in range(ASCENTS):
        last = ascent + 1 == ASCENTS
        emb = lax.optimization_barrier(emb_bf).astype(jnp.float32)
        inv_rms = lax.rsqrt(jnp.mean(emb * emb, axis=1, keepdims=True) + 1e-06)
        normed = (emb * inv_rms * norm_gain).astype(jnp.bfloat16)
        preact = jnp.dot(normed, weight_in, preferred_element_type=jnp.float32)
        hidden, slope = gelu_and_slope(preact)
        partial_value = jnp.dot(hidden, weight_out, preferred_element_type=jnp.float32)
        mixed = over_tensor(feature_blocks(partial_value.astype(jnp.bfloat16)))
        rights_out += [hidden, from_partner(hidden, "core")]
        lefts_in += for_both_cores(normed, core)
        out_grad = (embedded + mixed - target) * loss_scale
        grad = gathered_features(out_grad.astype(jnp.bfloat16))
        lefts_out += for_both_cores(grad, core)
        if last:
            partial_out = partial_over_chip(lefts_out, rights_out)
            slope = slope + nothing(partial_out[0, 0])
        hidden_grad = (
            jnp.dot(grad, weight_out.T, preferred_element_type=jnp.float32) * slope
        ).astype(jnp.bfloat16)
        rights_in += [hidden_grad, from_partner(hidden_grad, "core")]
        if not last:
            normed_partial = jnp.dot(hidden_grad, weight_in.T, preferred_element_type=jnp.float32)
            dot_partial = jnp.sum(normed_partial * norm_gain * emb, axis=1)
            dot_head = dot_partial.astype(jnp.bfloat16)
            dot_rest = (dot_partial - dot_head.astype(jnp.float32)).astype(jnp.bfloat16)
            dots = jnp.stack([dot_head, dot_rest], 1)[None]
            blocks = jnp.concatenate(
                [
                    feature_blocks(normed_partial.astype(jnp.bfloat16)),
                    jnp.broadcast_to(dots, (lax.axis_size(TENSOR), local_tokens, 2)),
                ],
                axis=2,
            )
            arrived = over_tensor(blocks)
            scaled = arrived[:, :width_local] * gain_local
            row_dot = jnp.sum(arrived[:, width_local:], axis=1, keepdims=True)
            emb_local = emb_local.astype(jnp.float32)
            delta_grad = (
                out_grad + inv_rms * scaled - emb_local * inv_rms * inv_rms * inv_rms * row_dot / D
            )
            delta_whole = gathered_features(delta_grad.astype(jnp.bfloat16)).astype(jnp.float32)
            row_squares = jnp.sum(delta_whole * delta_whole, axis=1)
            sums = jnp.stack(
                [jnp.sum(onehot * row_squares[:, None], axis=0), jnp.sum(onehot, axis=0)]
            )
            square_sums, counts = over_neighbours(sums)
            root_mean = jnp.sqrt(square_sums / (jnp.maximum(counts, 1.0) * D) + 1e-06)
            token_scale = jnp.sum(onehot * (adv_step / root_mean)[None, :], axis=1)[:, None]
            perturb = perturb + delta_grad * token_scale
            embedded = tokens.astype(jnp.float32) + perturb
            emb_bf = (emb + delta_whole * token_scale).astype(jnp.bfloat16)
    partial_in = partial_over_chip(lefts_in, rights_in)
    there = nothing(partial_in[0, 0])
    summed_out = summed_over_dp(partial_out, there, there)
    summed_in = summed_over_dp(partial_in, there, nothing(summed_out[0, 0]))
    summed_out = summed_out.T
    dp_rows = moment_in.shape[0]
    offset = lax.axis_index(DP) * dp_rows
    own_in = lax.dynamic_slice_in_dim(weight_in, offset, dp_rows, 0)
    own_out = lax.dynamic_slice_in_dim(weight_out, offset, dp_rows, 1)
    new_moment_in = decay * moment_in + summed_in / ASCENTS
    new_moment_out = decay * moment_out + summed_out / ASCENTS
    new_weight_in = (own_in.astype(jnp.float32) - learn_rate * new_moment_in).astype(jnp.bfloat16)
    new_weight_out = (own_out.astype(jnp.float32) - learn_rate * new_moment_out).astype(
        jnp.bfloat16
    )
    return (new_weight_in, new_weight_out, new_moment_in, new_moment_out, perturb)


def solution(mesh):
    torus = Mesh(mesh.devices.reshape(2, 4, 2, 4, 4), DP + TENSOR)
    in_specs = (
        P(DP, TENSOR),
        P(DP, TENSOR),
        P(DP),
        P(DP, TENSOR),
        P(),
        P(None, TENSOR),
        P(TENSOR, None),
        P(DP, TENSOR),
        P(TENSOR, DP),
    )
    out_specs = (P(DP, TENSOR), P(TENSOR, DP), P(DP, TENSOR), P(TENSOR, DP), P(DP, TENSOR))
    return jax.shard_map(
        shards, mesh=torus, in_specs=in_specs, out_specs=out_specs, check_vma=False
    )
```

```python
import jax
import jax.numpy as jnp
from jax import lax
from jax.sharding import Mesh
from jax.sharding import PartitionSpec as P

D = 1024
ASCENTS = 2
EXAMPLES = 32
DP = ("z_hi", "y", "core")
BLOCKS = ("z_hi", "y")
TENSOR = ("x", "z_lo")

coeff = 0.7978845608
adv_init = 0.5
adv_step = 0.5
decay = 0.9
learn_rate = 0.01


def to_peers(blocks, axis):
    return lax.all_to_all(blocks, axis, 0, 0, tiled=True)


def gathered_features(array):
    copies = jnp.broadcast_to(array, (lax.axis_size(TENSOR), *array.shape))
    blocks = to_peers(copies, TENSOR)
    return jnp.moveaxis(blocks, 0, 1).reshape(array.shape[0], -1)


def feature_blocks(array):
    return jnp.moveaxis(array.reshape(array.shape[0], lax.axis_size(TENSOR), -1), 1, 0)


def over_tensor(blocks):
    return jnp.sum(to_peers(blocks, TENSOR).astype(jnp.float32), axis=0)


def from_partner(array, axis):
    return lax.ppermute(array, axis, [(0, 1), (1, 0)])


def gelu_and_slope(values):
    tangent = jnp.tanh(coeff * (values + 0.044715 * values * values * values))
    value = 0.5 * values * (1.0 + tangent)
    slope = 0.5 * (1.0 + tangent) + 0.5 * values * (1.0 - tangent * tangent) * coeff * (
        1.0 + 3.0 * 0.044715 * values * values
    )
    return lax.optimization_barrier((value.astype(jnp.bfloat16), slope))


def over_neighbours(sums):
    count = lax.axis_size(BLOCKS)
    sums = sums + from_partner(sums, "core")
    before = lax.ppermute(sums, BLOCKS, [(i, i + 1) for i in range(count - 1)])
    after = lax.ppermute(sums, BLOCKS, [(i + 1, i) for i in range(count - 1)])
    return sums + before + after


LEAVING = ((0, 2), (1, 1), (1, 2), (0, 3), (0, 0), (1, 0), (0, 1), (1, 3))


def leaving_order(features, flip):
    z_hi, y, core = (lax.axis_index(name) for name in DP)
    n_y = lax.axis_size("y")
    width = features // (2 * len(LEAVING))
    blocks = [
        ((z_hi ^ far) * n_y + lax.rem(y + steps, n_y)) * 2 + (core ^ flip) for far, steps in LEAVING
    ]
    column = jnp.arange(features // 2, dtype=jnp.int32)
    source = column % width
    for place, block in enumerate(blocks):
        source = source + jnp.where(column // width == place, block * width, 0)
    return (jnp.arange(features, dtype=jnp.int32)[:, None] == source[None, :]).astype(jnp.bfloat16)


def for_both_cores(array, orders):
    own, other = [
        jnp.dot(array, order, preferred_element_type=jnp.float32).astype(jnp.bfloat16)
        for order in orders
    ]
    return [own, from_partner(other, "core")]


def over_y(partial, late):
    n_y = lax.axis_size("y")
    up = [(i, (i + 1) % n_y) for i in range(n_y)]
    down = [(i, (i - 1) % n_y) for i in range(n_y)]
    few = partial.shape[0] // len(LEAVING)

    def wide(array, place):
        return array[place * few : (place + 1) * few].astype(jnp.float32)

    risen = lax.ppermute(partial[: 2 * few], "y", up)
    sunk = lax.ppermute(partial[2 * few : 4 * few], "y", down)
    on_up = (wide(partial, 6) + wide(risen, 0) + late).astype(jnp.bfloat16)
    on_down = (wide(partial, 7) + wide(sunk, 0) + late).astype(jnp.bfloat16)
    on_up, on_down = lax.optimization_barrier((on_up, on_down))
    kept = wide(partial, 4) + wide(sunk, 1) + wide(lax.ppermute(on_up, "y", up), 0)
    other = wide(partial, 5) + wide(risen, 1) + wide(lax.ppermute(on_down, "y", down), 0)
    return kept, other


def nothing(value):
    return jnp.minimum(jnp.abs(value.astype(jnp.float32)), 0.0)


def partial_over_chip(lefts, rights):
    left, right = jnp.concatenate(lefts, 0), jnp.concatenate(rights, 0)
    return lax.dot_general(
        left, right, (((0,), (0,)), ((), ())), preferred_element_type=jnp.float32
    ).astype(jnp.bfloat16)


def summed_over_dp(partial, late_y, late_z):
    kept, other = over_y(partial, late_y)
    sent = (other + late_z).astype(jnp.bfloat16)
    return kept + from_partner(sent, "z_hi").astype(jnp.float32)


def shards(
    tokens, init_noise, segment_ids, target, norm_gain, weight_in, weight_out, moment_in, moment_out
):
    dp_count = lax.axis_size(DP)
    local_tokens, width_local = tokens.shape
    loss_scale = (local_tokens * dp_count) ** (-0.5)
    column = lax.axis_index(TENSOR)
    orders = [leaving_order(D, flip) for flip in (0, 1)]
    gain_local = lax.dynamic_slice_in_dim(norm_gain, column * width_local, width_local)
    labels = jnp.arange(EXAMPLES, dtype=jnp.int32)
    onehot = (segment_ids[:, None] == labels[None, :]).astype(jnp.float32)
    perturb = adv_init * init_noise
    embedded = tokens.astype(jnp.float32) + perturb
    emb_local = embedded.astype(jnp.bfloat16)
    emb_bf = gathered_features(emb_local)
    lefts_in, rights_in, lefts_out, rights_out = [], [], [], []
    for ascent in range(ASCENTS):
        last = ascent + 1 == ASCENTS
        emb = lax.optimization_barrier(emb_bf).astype(jnp.float32)
        inv_rms = lax.rsqrt(jnp.mean(emb * emb, axis=1, keepdims=True) + 1e-06)
        normed = (emb * inv_rms * norm_gain).astype(jnp.bfloat16)
        preact = jnp.dot(normed, weight_in, preferred_element_type=jnp.float32)
        hidden, slope = gelu_and_slope(preact)
        partial_value = jnp.dot(hidden, weight_out, preferred_element_type=jnp.float32)
        mixed = over_tensor(feature_blocks(partial_value.astype(jnp.bfloat16)))
        rights_out += [hidden, from_partner(hidden, "core")]
        lefts_in += for_both_cores(normed, orders)
        out_grad = (embedded + mixed - target) * loss_scale
        grad = gathered_features(out_grad.astype(jnp.bfloat16))
        lefts_out += for_both_cores(grad, orders)
        if last:
            partial_out = partial_over_chip(lefts_out, rights_out)
            slope = slope + nothing(partial_out[0, 0])
        hidden_grad = (
            jnp.dot(grad, weight_out.T, preferred_element_type=jnp.float32) * slope
        ).astype(jnp.bfloat16)
        rights_in += [hidden_grad, from_partner(hidden_grad, "core")]
        if not last:
            normed_partial = jnp.dot(hidden_grad, weight_in.T, preferred_element_type=jnp.float32)
            dot_partial = jnp.sum(normed_partial * norm_gain * emb, axis=1)
            dot_head = dot_partial.astype(jnp.bfloat16)
            dot_rest = (dot_partial - dot_head.astype(jnp.float32)).astype(jnp.bfloat16)
            dots = jnp.stack([dot_head, dot_rest], 1)[None]
            blocks = jnp.concatenate(
                [
                    feature_blocks(normed_partial.astype(jnp.bfloat16)),
                    jnp.broadcast_to(dots, (lax.axis_size(TENSOR), local_tokens, 2)),
                ],
                axis=2,
            )
            arrived = over_tensor(blocks)
            scaled = arrived[:, :width_local] * gain_local
            row_dot = jnp.sum(arrived[:, width_local:], axis=1, keepdims=True)
            emb_local = emb_local.astype(jnp.float32)
            delta_grad = (
                out_grad + inv_rms * scaled - emb_local * inv_rms * inv_rms * inv_rms * row_dot / D
            )
            delta_whole = gathered_features(delta_grad.astype(jnp.bfloat16)).astype(jnp.float32)
            row_squares = jnp.sum(delta_whole * delta_whole, axis=1)
            sums = jnp.stack(
                [jnp.sum(onehot * row_squares[:, None], axis=0), jnp.sum(onehot, axis=0)]
            )
            square_sums, counts = over_neighbours(sums)
            root_mean = jnp.sqrt(square_sums / (jnp.maximum(counts, 1.0) * D) + 1e-06)
            token_scale = jnp.sum(onehot * (adv_step / root_mean)[None, :], axis=1)[:, None]
            perturb = perturb + delta_grad * token_scale
            embedded = tokens.astype(jnp.float32) + perturb
            emb_bf = (emb + delta_whole * token_scale).astype(jnp.bfloat16)
    partial_in = partial_over_chip(lefts_in, rights_in)
    there = nothing(partial_in[0, 0])
    summed_out = summed_over_dp(partial_out, there, there)
    summed_in = summed_over_dp(partial_in, 0.0, nothing(summed_out[0, 0]))
    summed_out = summed_out.T
    dp_rows = moment_in.shape[0]
    offset = lax.axis_index(DP) * dp_rows
    own_in = lax.dynamic_slice_in_dim(weight_in, offset, dp_rows, 0)
    own_out = lax.dynamic_slice_in_dim(weight_out, offset, dp_rows, 1)
    new_moment_in = decay * moment_in + summed_in / ASCENTS
    new_moment_out = decay * moment_out + summed_out / ASCENTS
    new_weight_in = (own_in.astype(jnp.float32) - learn_rate * new_moment_in).astype(jnp.bfloat16)
    new_weight_out = (own_out.astype(jnp.float32) - learn_rate * new_moment_out).astype(
        jnp.bfloat16
    )
    return (new_weight_in, new_weight_out, new_moment_in, new_moment_out, perturb)


def solution(mesh):
    torus = Mesh(mesh.devices.reshape(2, 4, 2, 4, 4), DP + TENSOR)
    in_specs = (
        P(DP, TENSOR),
        P(DP, TENSOR),
        P(DP),
        P(DP, TENSOR),
        P(),
        P(None, TENSOR),
        P(TENSOR, None),
        P(DP, TENSOR),
        P(TENSOR, DP),
    )
    out_specs = (P(DP, TENSOR), P(TENSOR, DP), P(DP, TENSOR), P(TENSOR, DP), P(DP, TENSOR))
    return jax.shard_map(
        shards, mesh=torus, in_specs=in_specs, out_specs=out_specs, check_vma=False
    )
```

```python
import jax
import jax.numpy as jnp
from jax import lax
from jax.sharding import Mesh
from jax.sharding import PartitionSpec as P

D = 1024
ASCENTS = 2
EXAMPLES = 32
DP = ("z_hi", "y", "core")
BLOCKS = ("z_hi", "y")
TENSOR = ("x", "z_lo")

coeff = 0.7978845608
adv_init = 0.5
adv_step = 0.5
decay = 0.9
learn_rate = 0.01


def to_peers(blocks, axis):
    return lax.all_to_all(blocks, axis, 0, 0, tiled=True)


def gathered_features(array):
    copies = jnp.broadcast_to(array, (lax.axis_size(TENSOR), *array.shape))
    blocks = to_peers(copies, TENSOR)
    return jnp.moveaxis(blocks, 0, 1).reshape(array.shape[0], -1)


def feature_blocks(array):
    return jnp.moveaxis(array.reshape(array.shape[0], lax.axis_size(TENSOR), -1), 1, 0)


def over_tensor(blocks):
    return jnp.sum(to_peers(blocks, TENSOR).astype(jnp.float32), axis=0)


def from_partner(array, axis):
    return lax.ppermute(array, axis, [(0, 1), (1, 0)])


def gelu_and_slope(values):
    tangent = jnp.tanh(coeff * (values + 0.044715 * values * values * values))
    value = 0.5 * values * (1.0 + tangent)
    slope = 0.5 * (1.0 + tangent) + 0.5 * values * (1.0 - tangent * tangent) * coeff * (
        1.0 + 3.0 * 0.044715 * values * values
    )
    return lax.optimization_barrier((value.astype(jnp.bfloat16), slope))


def over_neighbours(sums):
    count = lax.axis_size(BLOCKS)
    sums = sums + from_partner(sums, "core")
    swaps = []
    for start in (1, 0):
        pairs = [(i, i + 1) for i in range(start, count - 1, 2)]
        swaps.append(lax.ppermute(sums, BLOCKS, pairs + [(j, i) for i, j in pairs]))
    return sums + swaps[0] + swaps[1]


LEAVING = ((0, 2), (1, 1), (1, 2), (0, 3), (0, 0), (1, 0), (0, 1), (1, 3))


def leaving_order(features, flip):
    z_hi, y, core = (lax.axis_index(name) for name in DP)
    n_y = lax.axis_size("y")
    width = features // (2 * len(LEAVING))
    blocks = [
        ((z_hi ^ far) * n_y + lax.rem(y + steps, n_y)) * 2 + (core ^ flip) for far, steps in LEAVING
    ]
    column = jnp.arange(features // 2, dtype=jnp.int32)
    source = column % width
    for place, block in enumerate(blocks):
        source = source + jnp.where(column // width == place, block * width, 0)
    return (jnp.arange(features, dtype=jnp.int32)[:, None] == source[None, :]).astype(jnp.bfloat16)


def for_both_cores(array, orders):
    own, other = [
        jnp.dot(array, order, preferred_element_type=jnp.float32).astype(jnp.bfloat16)
        for order in orders
    ]
    return [own, from_partner(other, "core")]


def over_y(partial, late):
    n_y = lax.axis_size("y")
    up = [(i, (i + 1) % n_y) for i in range(n_y)]
    down = [(i, (i - 1) % n_y) for i in range(n_y)]
    few = partial.shape[0] // len(LEAVING)

    def wide(array, place):
        return array[place * few : (place + 1) * few].astype(jnp.float32)

    risen = lax.ppermute(partial[: 2 * few], "y", up)
    sunk = lax.ppermute(partial[2 * few : 4 * few], "y", down)
    on_up = (wide(partial, 6) + wide(risen, 0) + late).astype(jnp.bfloat16)
    on_down = (wide(partial, 7) + wide(sunk, 0) + late).astype(jnp.bfloat16)
    on_up, on_down = lax.optimization_barrier((on_up, on_down))
    kept = wide(partial, 4) + wide(sunk, 1) + wide(lax.ppermute(on_up, "y", up), 0)
    other = wide(partial, 5) + wide(risen, 1) + wide(lax.ppermute(on_down, "y", down), 0)
    return kept, other


def nothing(value):
    return jnp.minimum(jnp.abs(value.astype(jnp.float32)), 0.0)


def partial_over_chip(lefts, rights):
    left, right = jnp.concatenate(lefts, 0), jnp.concatenate(rights, 0)
    return lax.dot_general(
        left, right, (((0,), (0,)), ((), ())), preferred_element_type=jnp.float32
    ).astype(jnp.bfloat16)


def summed_over_dp(partial, late_y, late_z):
    kept, other = over_y(partial, late_y)
    arrived = from_partner((other + late_z).astype(jnp.bfloat16), "z_hi")
    return kept + arrived.astype(jnp.float32), nothing(arrived[0, 0])


def shards(
    tokens, init_noise, segment_ids, target, norm_gain, weight_in, weight_out, moment_in, moment_out
):
    dp_count = lax.axis_size(DP)
    local_tokens, width_local = tokens.shape
    loss_scale = (local_tokens * dp_count) ** (-0.5)
    column = lax.axis_index(TENSOR)
    orders = [leaving_order(D, flip) for flip in (0, 1)]
    gain_local = lax.dynamic_slice_in_dim(norm_gain, column * width_local, width_local)
    labels = jnp.arange(EXAMPLES, dtype=jnp.int32)
    onehot = (segment_ids[:, None] == labels[None, :]).astype(jnp.float32)
    perturb = adv_init * init_noise
    embedded = tokens.astype(jnp.float32) + perturb
    emb_local = embedded.astype(jnp.bfloat16)
    emb_bf = gathered_features(emb_local)
    lefts_in, rights_in, lefts_out, rights_out = [], [], [], []
    for ascent in range(ASCENTS):
        last = ascent + 1 == ASCENTS
        emb = lax.optimization_barrier(emb_bf).astype(jnp.float32)
        inv_rms = lax.rsqrt(jnp.mean(emb * emb, axis=1, keepdims=True) + 1e-06)
        normed = (emb * inv_rms * norm_gain).astype(jnp.bfloat16)
        preact = jnp.dot(normed, weight_in, preferred_element_type=jnp.float32)
        hidden, slope = gelu_and_slope(preact)
        partial_value = jnp.dot(hidden, weight_out, preferred_element_type=jnp.float32)
        mixed = over_tensor(feature_blocks(partial_value.astype(jnp.bfloat16)))
        rights_out += [hidden, from_partner(hidden, "core")]
        lefts_in += for_both_cores(normed, orders)
        out_grad = (embedded + mixed - target) * loss_scale
        grad = gathered_features(out_grad.astype(jnp.bfloat16))
        lefts_out += for_both_cores(grad, orders)
        if last:
            partial_out = partial_over_chip(lefts_out, rights_out)
            slope = slope + nothing(partial_out[0, 0])
        hidden_grad = (
            jnp.dot(grad, weight_out.T, preferred_element_type=jnp.float32) * slope
        ).astype(jnp.bfloat16)
        rights_in += [hidden_grad, from_partner(hidden_grad, "core")]
        if not last:
            normed_partial = jnp.dot(hidden_grad, weight_in.T, preferred_element_type=jnp.float32)
            dot_partial = jnp.sum(normed_partial * norm_gain * emb, axis=1)
            dot_head = dot_partial.astype(jnp.bfloat16)
            dot_rest = (dot_partial - dot_head.astype(jnp.float32)).astype(jnp.bfloat16)
            dots = jnp.stack([dot_head, dot_rest], 1)[None]
            blocks = jnp.concatenate(
                [
                    feature_blocks(normed_partial.astype(jnp.bfloat16)),
                    jnp.broadcast_to(dots, (lax.axis_size(TENSOR), local_tokens, 2)),
                ],
                axis=2,
            )
            arrived = over_tensor(blocks)
            scaled = arrived[:, :width_local] * gain_local
            row_dot = jnp.sum(arrived[:, width_local:], axis=1, keepdims=True)
            emb_local = emb_local.astype(jnp.float32)
            delta_grad = (
                out_grad + inv_rms * scaled - emb_local * inv_rms * inv_rms * inv_rms * row_dot / D
            )
            delta_whole = gathered_features(delta_grad.astype(jnp.bfloat16)).astype(jnp.float32)
            row_squares = jnp.sum(delta_whole * delta_whole, axis=1)
            sums = jnp.stack(
                [jnp.sum(onehot * row_squares[:, None], axis=0), jnp.sum(onehot, axis=0)]
            )
            square_sums, counts = over_neighbours(sums)
            root_mean = jnp.sqrt(square_sums / (jnp.maximum(counts, 1.0) * D) + 1e-06)
            token_scale = jnp.sum(onehot * (adv_step / root_mean)[None, :], axis=1)[:, None]
            perturb = perturb + delta_grad * token_scale
            embedded = tokens.astype(jnp.float32) + perturb
            emb_bf = (emb + delta_whole * token_scale).astype(jnp.bfloat16)
    partial_in = partial_over_chip(lefts_in, rights_in)
    there = nothing(partial_in[0, 0])
    summed_out, there = summed_over_dp(partial_out, there, there)
    summed_in, _ = summed_over_dp(partial_in, 0.0, there)
    summed_out = summed_out.T
    dp_rows = moment_in.shape[0]
    offset = lax.axis_index(DP) * dp_rows
    own_in = lax.dynamic_slice_in_dim(weight_in, offset, dp_rows, 0)
    own_out = lax.dynamic_slice_in_dim(weight_out, offset, dp_rows, 1)
    new_moment_in = decay * moment_in + summed_in / ASCENTS
    new_moment_out = decay * moment_out + summed_out / ASCENTS
    new_weight_in = (own_in.astype(jnp.float32) - learn_rate * new_moment_in).astype(jnp.bfloat16)
    new_weight_out = (own_out.astype(jnp.float32) - learn_rate * new_moment_out).astype(
        jnp.bfloat16
    )
    return (new_weight_in, new_weight_out, new_moment_in, new_moment_out, perturb)


def solution(mesh):
    torus = Mesh(mesh.devices.reshape(2, 4, 2, 4, 4), DP + TENSOR)
    in_specs = (
        P(DP, TENSOR),
        P(DP, TENSOR),
        P(DP),
        P(DP, TENSOR),
        P(),
        P(None, TENSOR),
        P(TENSOR, None),
        P(DP, TENSOR),
        P(TENSOR, DP),
    )
    out_specs = (P(DP, TENSOR), P(TENSOR, DP), P(DP, TENSOR), P(TENSOR, DP), P(DP, TENSOR))
    return jax.shard_map(
        shards, mesh=torus, in_specs=in_specs, out_specs=out_specs, check_vma=False
    )
```

```python
import jax
import jax.numpy as jnp
from jax import lax
from jax.sharding import Mesh
from jax.sharding import PartitionSpec as P

D = 1024
ASCENTS = 2
EXAMPLES = 32
DP = ("z_hi", "y", "core")
BLOCKS = ("z_hi", "y")
TENSOR = ("x", "z_lo")

coeff = 0.7978845608
adv_init = 0.5
adv_step = 0.5
decay = 0.9
learn_rate = 0.01


def to_peers(blocks, axis):
    return lax.all_to_all(blocks, axis, 0, 0, tiled=True)


def gathered_features(array):
    copies = jnp.broadcast_to(array, (lax.axis_size(TENSOR), *array.shape))
    blocks = to_peers(copies, TENSOR)
    return jnp.moveaxis(blocks, 0, 1).reshape(array.shape[0], -1)


def feature_blocks(array):
    return jnp.moveaxis(array.reshape(array.shape[0], lax.axis_size(TENSOR), -1), 1, 0)


def over_tensor(blocks):
    return jnp.sum(to_peers(blocks, TENSOR).astype(jnp.float32), axis=0)


def from_partner(array, axis):
    return lax.ppermute(array, axis, [(0, 1), (1, 0)])


def gelu_and_slope(values):
    square = values * values
    share = 0.5 * jnp.tanh(coeff * values * (1.0 + 0.044715 * square)) + 0.5
    value = values * share
    slope = share + 2.0 * share * (1.0 - share) * values * coeff * (1.0 + 3.0 * 0.044715 * square)
    return lax.optimization_barrier((value.astype(jnp.bfloat16), slope))


def over_neighbours(sums):
    count = lax.axis_size(BLOCKS)
    sums = sums + from_partner(sums, "core")
    swaps = []
    for start in (1, 0):
        pairs = [(i, i + 1) for i in range(start, count - 1, 2)]
        swaps.append(lax.ppermute(sums, BLOCKS, pairs + [(j, i) for i, j in pairs]))
    return sums + swaps[0] + swaps[1]


LEAVING = ((0, 2), (1, 1), (1, 2), (0, 3), (0, 0), (1, 0), (0, 1), (1, 3))


def leaving_order(features, flip):
    z_hi, y, core = (lax.axis_index(name) for name in DP)
    n_y = lax.axis_size("y")
    width = features // (2 * len(LEAVING))
    blocks = [
        ((z_hi ^ far) * n_y + lax.rem(y + steps, n_y)) * 2 + (core ^ flip) for far, steps in LEAVING
    ]
    column = jnp.arange(features // 2, dtype=jnp.int32)
    source = column % width
    for place, block in enumerate(blocks):
        source = source + jnp.where(column // width == place, block * width, 0)
    return (jnp.arange(features, dtype=jnp.int32)[:, None] == source[None, :]).astype(jnp.bfloat16)


def for_both_cores(array, orders):
    own, other = [
        jnp.dot(array, order, preferred_element_type=jnp.float32).astype(jnp.bfloat16)
        for order in orders
    ]
    return [own, from_partner(other, "core")]


def along_y(message, step):
    n_y = lax.axis_size("y")
    return lax.ppermute(message, "y", [(i, (i + step) % n_y) for i in range(n_y)])


def runs(array, *places):
    few = D // 2 // len(LEAVING)
    return [array[place * few : (place + 1) * few].astype(jnp.float32) for place in places]


def first_step(partial, wide):
    few = D // 2 // len(LEAVING)
    sizes = 2 * few if wide else few
    return along_y(partial[:sizes], 1), along_y(partial[2 * few : 2 * few + sizes], -1)


def second_step(partial, risen, sunk, late, wide):
    up_later, up, down_later, down, kept, other, near_up, near_down = runs(partial, *range(8))
    near_up = near_up + runs(risen, 0)[0] + late[0]
    near_down = near_down + runs(sunk, 0)[0] + late[1]
    if wide:
        near_down = near_down + nothing(runs(risen, 0)[0])
        up, down = runs(risen, 1)[0], runs(sunk, 1)[0]
        near_up = runs(along_y(near_up.astype(jnp.bfloat16), 1), 0)[0]
        near_down = runs(along_y(near_down.astype(jnp.bfloat16), -1), 0)[0]
    else:
        above = along_y(jnp.concatenate([near_up, up]).astype(jnp.bfloat16), 1)
        below = along_y(jnp.concatenate([near_down, down]).astype(jnp.bfloat16), -1)
        near_up, up = runs(above, 0, 1)
        near_down, down = runs(below, 0, 1)
    return kept + near_up + down, other + near_down + up


def nothing(value):
    return jnp.minimum(jnp.abs(value.astype(jnp.float32)), 0.0)


def partial_over_chip(lefts, rights):
    left, right = jnp.concatenate(lefts, 0), jnp.concatenate(rights, 0)
    return lax.dot_general(
        left, right, (((0,), (0,)), ((), ())), preferred_element_type=jnp.float32
    ).astype(jnp.bfloat16)


def over_z(sums, late):
    kept, other = sums
    arrived = from_partner((other + late).astype(jnp.bfloat16), "z_hi")
    return kept + arrived.astype(jnp.float32), nothing(arrived)


def shards(
    tokens, init_noise, segment_ids, target, norm_gain, weight_in, weight_out, moment_in, moment_out
):
    dp_count = lax.axis_size(DP)
    local_tokens, width_local = tokens.shape
    loss_scale = (local_tokens * dp_count) ** (-0.5)
    column = lax.axis_index(TENSOR)
    orders = [leaving_order(D, flip) for flip in (0, 1)]
    gain_local = lax.dynamic_slice_in_dim(norm_gain, column * width_local, width_local)
    labels = jnp.arange(EXAMPLES, dtype=jnp.int32)
    onehot = (segment_ids[:, None] == labels[None, :]).astype(jnp.float32)
    perturb = adv_init * init_noise
    embedded = tokens.astype(jnp.float32) + perturb
    emb_local = embedded.astype(jnp.bfloat16)
    emb_bf = gathered_features(emb_local)
    lefts_in, rights_in, lefts_out, rights_out = [], [], [], []
    for ascent in range(ASCENTS):
        last = ascent + 1 == ASCENTS
        emb = lax.optimization_barrier(emb_bf).astype(jnp.float32)
        inv_rms = lax.rsqrt(jnp.mean(emb * emb, axis=1, keepdims=True) + 1e-06)
        normed = (emb * inv_rms * norm_gain).astype(jnp.bfloat16)
        preact = jnp.dot(normed, weight_in, preferred_element_type=jnp.float32)
        hidden, slope = gelu_and_slope(preact)
        partial_value = jnp.dot(hidden, weight_out, preferred_element_type=jnp.float32)
        mixed = over_tensor(feature_blocks(partial_value.astype(jnp.bfloat16)))
        rights_out += [hidden, from_partner(hidden, "core")]
        lefts_in += for_both_cores(normed, orders)
        out_grad = (embedded + mixed - target) * loss_scale
        grad = gathered_features(out_grad.astype(jnp.bfloat16))
        lefts_out += for_both_cores(grad, orders)
        if last:
            partial_out = partial_over_chip(lefts_out, rights_out)
            slope = slope + nothing(partial_out[0, 0])
        hidden_grad = (
            jnp.dot(grad, weight_out.T, preferred_element_type=jnp.float32) * slope
        ).astype(jnp.bfloat16)
        rights_in += [hidden_grad, from_partner(hidden_grad, "core")]
        if not last:
            normed_partial = jnp.dot(hidden_grad, weight_in.T, preferred_element_type=jnp.float32)
            dot_partial = jnp.sum(normed_partial * norm_gain * emb, axis=1)
            dot_head = dot_partial.astype(jnp.bfloat16)
            dot_rest = (dot_partial - dot_head.astype(jnp.float32)).astype(jnp.bfloat16)
            dots = jnp.stack([dot_head, dot_rest], 1)[None]
            blocks = jnp.concatenate(
                [
                    feature_blocks(normed_partial.astype(jnp.bfloat16)),
                    jnp.broadcast_to(dots, (lax.axis_size(TENSOR), local_tokens, 2)),
                ],
                axis=2,
            )
            arrived = over_tensor(blocks)
            scaled = arrived[:, :width_local] * gain_local
            row_dot = jnp.sum(arrived[:, width_local:], axis=1, keepdims=True)
            emb_local = emb_local.astype(jnp.float32)
            delta_grad = (
                out_grad + inv_rms * scaled - emb_local * inv_rms * inv_rms * inv_rms * row_dot / D
            )
            delta_whole = gathered_features(delta_grad.astype(jnp.bfloat16)).astype(jnp.float32)
            row_squares = jnp.sum(delta_whole * delta_whole, axis=1)
            sums = jnp.stack(
                [jnp.sum(onehot * row_squares[:, None], axis=0), jnp.sum(onehot, axis=0)]
            )
            square_sums, counts = over_neighbours(sums)
            root_mean = jnp.sqrt(square_sums / (jnp.maximum(counts, 1.0) * D) + 1e-06)
            token_scale = jnp.sum(onehot * (adv_step / root_mean)[None, :], axis=1)[:, None]
            perturb = perturb + delta_grad * token_scale
            embedded = tokens.astype(jnp.float32) + perturb
            emb_bf = (emb + delta_whole * token_scale).astype(jnp.bfloat16)
    partial_in = partial_over_chip(lefts_in, rights_in)
    sent_out, sent_in = first_step(partial_out, True), first_step(partial_in, False)
    there = [nothing(message) for message in sent_in]
    sums_out = second_step(partial_out, *sent_out, there, True)
    sums_in = second_step(partial_in, *sent_in, (0.0, 0.0), False)
    summed_out, there = over_z(sums_out, 0.0)
    summed_in, _ = over_z(sums_in, there)
    summed_out = summed_out.T
    dp_rows = moment_in.shape[0]
    offset = lax.axis_index(DP) * dp_rows
    own_in = lax.dynamic_slice_in_dim(weight_in, offset, dp_rows, 0)
    own_out = lax.dynamic_slice_in_dim(weight_out, offset, dp_rows, 1)
    new_moment_in = decay * moment_in + summed_in / ASCENTS
    new_moment_out = decay * moment_out + summed_out / ASCENTS
    new_weight_in = (own_in.astype(jnp.float32) - learn_rate * new_moment_in).astype(jnp.bfloat16)
    new_weight_out = (own_out.astype(jnp.float32) - learn_rate * new_moment_out).astype(
        jnp.bfloat16
    )
    return (new_weight_in, new_weight_out, new_moment_in, new_moment_out, perturb)


def solution(mesh):
    torus = Mesh(mesh.devices.reshape(2, 4, 2, 4, 4), DP + TENSOR)
    in_specs = (
        P(DP, TENSOR),
        P(DP, TENSOR),
        P(DP),
        P(DP, TENSOR),
        P(),
        P(None, TENSOR),
        P(TENSOR, None),
        P(DP, TENSOR),
        P(TENSOR, DP),
    )
    out_specs = (P(DP, TENSOR), P(TENSOR, DP), P(DP, TENSOR), P(TENSOR, DP), P(DP, TENSOR))
    return jax.shard_map(
        shards, mesh=torus, in_specs=in_specs, out_specs=out_specs, check_vma=False
    )
```

```python
import jax
import jax.numpy as jnp
from jax import lax
from jax.sharding import Mesh
from jax.sharding import PartitionSpec as P

D = 1024
ASCENTS = 2
EXAMPLES = 32
DP = ("z_hi", "y", "core")
BLOCKS = ("z_hi", "y")
TENSOR = ("x", "z_lo")

coeff = 0.7978845608
adv_init = 0.5
adv_step = 0.5
decay = 0.9
learn_rate = 0.01


def to_peers(blocks, axis):
    return lax.all_to_all(blocks, axis, 0, 0, tiled=True)


def gathered_features(array):
    copies = jnp.broadcast_to(array, (lax.axis_size(TENSOR), *array.shape))
    blocks = to_peers(copies, TENSOR)
    return jnp.moveaxis(blocks, 0, 1).reshape(array.shape[0], -1)


def feature_blocks(array):
    return jnp.moveaxis(array.reshape(array.shape[0], lax.axis_size(TENSOR), -1), 1, 0)


def over_tensor(blocks):
    return jnp.sum(to_peers(blocks, TENSOR).astype(jnp.float32), axis=0)


def from_partner(array, axis):
    return lax.ppermute(array, axis, [(0, 1), (1, 0)])


def gelu_and_slope(values):
    square = values * values
    share = 0.5 * jnp.tanh(coeff * values * (1.0 + 0.044715 * square)) + 0.5
    value = values * share
    slope = share + 2.0 * share * (1.0 - share) * values * coeff * (1.0 + 3.0 * 0.044715 * square)
    return lax.optimization_barrier((value.astype(jnp.bfloat16), slope))


def over_neighbours(sums):
    count = lax.axis_size(BLOCKS)
    sums = sums + from_partner(sums, "core")
    swaps = []
    for start in (1, 0):
        pairs = [(i, i + 1) for i in range(start, count - 1, 2)]
        swaps.append(lax.ppermute(sums, BLOCKS, pairs + [(j, i) for i, j in pairs]))
    return sums + swaps[0] + swaps[1]


LEAVING = ((0, 2), (1, 1), (1, 2), (0, 3), (0, 0), (1, 0), (0, 1), (1, 3))


def leaving_order(features, flip):
    z_hi, y, core = (lax.axis_index(name) for name in DP)
    n_y = lax.axis_size("y")
    width = features // (2 * len(LEAVING))
    blocks = [
        ((z_hi ^ far) * n_y + lax.rem(y + steps, n_y)) * 2 + (core ^ flip) for far, steps in LEAVING
    ]
    column = jnp.arange(features // 2, dtype=jnp.int32)
    source = column % width
    for place, block in enumerate(blocks):
        source = source + jnp.where(column // width == place, block * width, 0)
    return (jnp.arange(features, dtype=jnp.int32)[:, None] == source[None, :]).astype(jnp.bfloat16)


def for_both_cores(array, orders):
    own, other = [
        jnp.dot(array, order, preferred_element_type=jnp.float32).astype(jnp.bfloat16)
        for order in orders
    ]
    return [own, from_partner(other, "core")]


def along_y(message, step):
    n_y = lax.axis_size("y")
    return lax.ppermute(message, "y", [(i, (i + step) % n_y) for i in range(n_y)])


def runs(array, *places):
    few = D // 2 // len(LEAVING)
    return [array[place * few : (place + 1) * few].astype(jnp.float32) for place in places]


def first_step(partial, wide):
    few = D // 2 // len(LEAVING)
    sizes = 2 * few if wide else few
    return along_y(partial[:sizes], 1), along_y(partial[2 * few : 2 * few + sizes], -1)


def second_step(partial, risen, sunk, late, wide):
    up_later, up, down_later, down, kept, other, near_up, near_down = runs(partial, *range(8))
    near_up = near_up + runs(lax.optimization_barrier(risen), 0)[0] + late[0]
    near_down = near_down + runs(sunk, 0)[0]
    if wide:
        near_down = near_down + nothing(runs(risen, 0)[0])
        up, down = runs(risen, 1)[0], runs(sunk, 1)[0]
        near_up = runs(along_y(near_up.astype(jnp.bfloat16), 1), 0)[0]
        near_down = runs(along_y(near_down.astype(jnp.bfloat16), -1), 0)[0]
    else:
        above = along_y(jnp.concatenate([near_up, up]).astype(jnp.bfloat16), 1)
        below = along_y(jnp.concatenate([near_down, down]).astype(jnp.bfloat16), -1)
        near_up, up = runs(above, 0, 1)
        near_down, down = runs(below, 0, 1)
    return kept + near_up + down, other + near_down + up


def nothing(value):
    return jnp.minimum(jnp.abs(value.astype(jnp.float32)), 0.0)


def partial_over_chip(lefts, rights):
    left, right = jnp.concatenate(lefts, 0), jnp.concatenate(rights, 0)
    return lax.dot_general(
        left, right, (((0,), (0,)), ((), ())), preferred_element_type=jnp.float32
    ).astype(jnp.bfloat16)


def over_z(sums, late):
    kept, other = sums
    arrived = from_partner((other + late).astype(jnp.bfloat16), "z_hi")
    return kept + arrived.astype(jnp.float32), nothing(arrived)


def shards(
    tokens, init_noise, segment_ids, target, norm_gain, weight_in, weight_out, moment_in, moment_out
):
    dp_count = lax.axis_size(DP)
    local_tokens, width_local = tokens.shape
    loss_scale = (local_tokens * dp_count) ** (-0.5)
    column = lax.axis_index(TENSOR)
    orders = [leaving_order(D, flip) for flip in (0, 1)]
    gain_local = lax.dynamic_slice_in_dim(norm_gain, column * width_local, width_local)
    labels = jnp.arange(EXAMPLES, dtype=jnp.int32)
    onehot = (segment_ids[:, None] == labels[None, :]).astype(jnp.float32)
    perturb = adv_init * init_noise
    embedded = tokens.astype(jnp.float32) + perturb
    emb_local = embedded.astype(jnp.bfloat16)
    emb_bf = gathered_features(emb_local)
    lefts_in, rights_in, lefts_out, rights_out = [], [], [], []
    for ascent in range(ASCENTS):
        last = ascent + 1 == ASCENTS
        emb = lax.optimization_barrier(emb_bf).astype(jnp.float32)
        inv_rms = lax.rsqrt(jnp.mean(emb * emb, axis=1, keepdims=True) + 1e-06)
        normed = (emb * inv_rms * norm_gain).astype(jnp.bfloat16)
        preact = jnp.dot(normed, weight_in, preferred_element_type=jnp.float32)
        hidden, slope = gelu_and_slope(preact)
        partial_value = jnp.dot(hidden, weight_out, preferred_element_type=jnp.float32)
        mixed = over_tensor(feature_blocks(partial_value.astype(jnp.bfloat16)))
        rights_out += [hidden, from_partner(hidden, "core")]
        lefts_in += for_both_cores(normed, orders)
        out_grad = (embedded + mixed - target) * loss_scale
        grad = gathered_features(out_grad.astype(jnp.bfloat16))
        lefts_out += for_both_cores(grad, orders)
        if last:
            partial_out = partial_over_chip(lefts_out, rights_out)
            slope = slope + nothing(partial_out[:local_tokens])
        hidden_grad = (
            jnp.dot(grad, weight_out.T, preferred_element_type=jnp.float32) * slope
        ).astype(jnp.bfloat16)
        rights_in += [hidden_grad, from_partner(hidden_grad, "core")]
        if not last:
            normed_partial = jnp.dot(hidden_grad, weight_in.T, preferred_element_type=jnp.float32)
            dot_partial = jnp.sum(normed_partial * norm_gain * emb, axis=1)
            dot_head = dot_partial.astype(jnp.bfloat16)
            dot_rest = (dot_partial - dot_head.astype(jnp.float32)).astype(jnp.bfloat16)
            dots = jnp.stack([dot_head, dot_rest], 1)[None]
            blocks = jnp.concatenate(
                [
                    feature_blocks(normed_partial.astype(jnp.bfloat16)),
                    jnp.broadcast_to(dots, (lax.axis_size(TENSOR), local_tokens, 2)),
                ],
                axis=2,
            )
            arrived = over_tensor(blocks)
            scaled = arrived[:, :width_local] * gain_local
            row_dot = jnp.sum(arrived[:, width_local:], axis=1, keepdims=True)
            emb_local = emb_local.astype(jnp.float32)
            delta_grad = (
                out_grad + inv_rms * scaled - emb_local * inv_rms * inv_rms * inv_rms * row_dot / D
            )
            delta_whole = gathered_features(delta_grad.astype(jnp.bfloat16)).astype(jnp.float32)
            row_squares = jnp.sum(delta_whole * delta_whole, axis=1)
            sums = jnp.stack(
                [jnp.sum(onehot * row_squares[:, None], axis=0), jnp.sum(onehot, axis=0)]
            )
            square_sums, counts = over_neighbours(sums)
            root_mean = jnp.sqrt(square_sums / (jnp.maximum(counts, 1.0) * D) + 1e-06)
            token_scale = jnp.sum(onehot * (adv_step / root_mean)[None, :], axis=1)[:, None]
            perturb = perturb + delta_grad * token_scale
            embedded = tokens.astype(jnp.float32) + perturb
            emb_bf = (emb + delta_whole * token_scale).astype(jnp.bfloat16)
    partial_in = partial_over_chip(lefts_in, rights_in)
    sent_out, sent_in = first_step(partial_out, True), first_step(partial_in, False)
    there = [nothing(message) for message in sent_in]
    sums_out = second_step(partial_out, *sent_out, there, True)
    sums_in = second_step(partial_in, *sent_in, (0.0, 0.0), False)
    summed_out, there = over_z(sums_out, 0.0)
    summed_in, _ = over_z(sums_in, there)
    summed_out = summed_out.T
    dp_rows = moment_in.shape[0]
    offset = lax.axis_index(DP) * dp_rows
    own_in = lax.dynamic_slice_in_dim(weight_in, offset, dp_rows, 0)
    own_out = lax.dynamic_slice_in_dim(weight_out, offset, dp_rows, 1)
    new_moment_in = decay * moment_in + summed_in / ASCENTS
    new_moment_out = decay * moment_out + summed_out / ASCENTS
    new_weight_in = (own_in.astype(jnp.float32) - learn_rate * new_moment_in).astype(jnp.bfloat16)
    new_weight_out = (own_out.astype(jnp.float32) - learn_rate * new_moment_out).astype(
        jnp.bfloat16
    )
    return (new_weight_in, new_weight_out, new_moment_in, new_moment_out, perturb)


def solution(mesh):
    torus = Mesh(mesh.devices.reshape(2, 4, 2, 4, 4), DP + TENSOR)
    in_specs = (
        P(DP, TENSOR),
        P(DP, TENSOR),
        P(DP),
        P(DP, TENSOR),
        P(),
        P(None, TENSOR),
        P(TENSOR, None),
        P(DP, TENSOR),
        P(TENSOR, DP),
    )
    out_specs = (P(DP, TENSOR), P(TENSOR, DP), P(DP, TENSOR), P(TENSOR, DP), P(DP, TENSOR))
    return jax.shard_map(
        shards, mesh=torus, in_specs=in_specs, out_specs=out_specs, check_vma=False
    )
```

```python
import jax
import jax.numpy as jnp
from jax import lax
from jax.sharding import Mesh
from jax.sharding import PartitionSpec as P

D = 1024
ASCENTS = 2
EXAMPLES = 32
DP = ("z_hi", "y", "core")
BLOCKS = ("z_hi", "y")
TENSOR = ("x", "z_lo")

coeff = 0.7978845608
adv_init = 0.5
adv_step = 0.5
decay = 0.9
learn_rate = 0.01


def to_peers(blocks, axis):
    return lax.all_to_all(blocks, axis, 0, 0, tiled=True)


def gathered_features(array):
    copies = jnp.broadcast_to(array, (lax.axis_size(TENSOR), *array.shape))
    blocks = to_peers(copies, TENSOR)
    return jnp.moveaxis(blocks, 0, 1).reshape(array.shape[0], -1)


def feature_blocks(array):
    return jnp.moveaxis(array.reshape(array.shape[0], lax.axis_size(TENSOR), -1), 1, 0)


def over_tensor(blocks):
    return jnp.sum(to_peers(blocks, TENSOR).astype(jnp.float32), axis=0)


def from_partner(array, axis):
    return lax.ppermute(array, axis, [(0, 1), (1, 0)])


def gelu_and_slope(values):
    square = values * values
    share = 0.5 * jnp.tanh(coeff * values * (1.0 + 0.044715 * square)) + 0.5
    value = values * share
    slope = share + 2.0 * share * (1.0 - share) * values * coeff * (1.0 + 3.0 * 0.044715 * square)
    return lax.optimization_barrier((value.astype(jnp.bfloat16), slope))


def over_neighbours(sums):
    count = lax.axis_size(BLOCKS)
    sums = sums + from_partner(sums, "core")
    swaps = []
    for start in (1, 0):
        pairs = [(i, i + 1) for i in range(start, count - 1, 2)]
        swaps.append(lax.ppermute(sums, BLOCKS, pairs + [(j, i) for i, j in pairs]))
    return sums + swaps[0] + swaps[1]


LEAVING = ((0, 2), (1, 1), (1, 2), (0, 3), (0, 0), (1, 0), (0, 1), (1, 3))


def leaving_order(features, flip):
    z_hi, y, core = (lax.axis_index(name) for name in DP)
    n_y = lax.axis_size("y")
    width = features // (2 * len(LEAVING))
    blocks = [
        ((z_hi ^ far) * n_y + lax.rem(y + steps, n_y)) * 2 + (core ^ flip) for far, steps in LEAVING
    ]
    column = jnp.arange(features // 2, dtype=jnp.int32)
    source = column % width
    for place, block in enumerate(blocks):
        source = source + jnp.where(column // width == place, block * width, 0)
    return (jnp.arange(features, dtype=jnp.int32)[:, None] == source[None, :]).astype(jnp.bfloat16)


def for_both_cores(array, orders):
    own, other = [
        jnp.dot(array, order, preferred_element_type=jnp.float32).astype(jnp.bfloat16)
        for order in orders
    ]
    return [own, from_partner(other, "core")]


def along_y(message, step):
    n_y = lax.axis_size("y")
    return lax.ppermute(message, "y", [(i, (i + step) % n_y) for i in range(n_y)])


def runs(array, *places):
    few = D // 2 // len(LEAVING)
    return [array[place * few : (place + 1) * few].astype(jnp.float32) for place in places]


def first_step(partial, wide):
    few = D // 2 // len(LEAVING)
    sizes = 2 * few if wide else few
    return along_y(partial[:sizes], 1), along_y(partial[2 * few : 2 * few + sizes], -1)


def second_step(partial, risen, sunk, late, wide):
    up_later, up, down_later, down, kept, other, near_up, near_down = runs(partial, *range(8))
    near_up = near_up + runs(risen, 0)[0] + late[0]
    near_down = near_down + runs(sunk, 0)[0] + late[1]
    if wide:
        near_down = near_down + nothing(runs(risen, 0)[0])
        up, down = runs(risen, 1)[0], runs(sunk, 1)[0]
    else:
        up, down = [
            runs(along_y(array.astype(jnp.bfloat16), step), 0)[0]
            for array, step in ((up, 1), (down, -1))
        ]
    near_up = runs(along_y(near_up.astype(jnp.bfloat16), 1), 0)[0]
    near_down = runs(along_y(near_down.astype(jnp.bfloat16), -1), 0)[0]
    return kept + near_up + down, other + near_down + up


def nothing(value):
    return jnp.minimum(jnp.abs(value.astype(jnp.float32)), 0.0)


def partial_over_chip(lefts, rights):
    left, right = jnp.concatenate(lefts, 0), jnp.concatenate(rights, 0)
    return lax.dot_general(
        left, right, (((0,), (0,)), ((), ())), preferred_element_type=jnp.float32
    ).astype(jnp.bfloat16)


def over_z(sums, late):
    kept, other = sums
    arrived = from_partner((other + late).astype(jnp.bfloat16), "z_hi")
    return kept + arrived.astype(jnp.float32), nothing(arrived)


def shards(
    tokens, init_noise, segment_ids, target, norm_gain, weight_in, weight_out, moment_in, moment_out
):
    dp_count = lax.axis_size(DP)
    local_tokens, width_local = tokens.shape
    loss_scale = (local_tokens * dp_count) ** (-0.5)
    column = lax.axis_index(TENSOR)
    orders = [leaving_order(D, flip) for flip in (0, 1)]
    gain_local = lax.dynamic_slice_in_dim(norm_gain, column * width_local, width_local)
    labels = jnp.arange(EXAMPLES, dtype=jnp.int32)
    onehot = (segment_ids[:, None] == labels[None, :]).astype(jnp.float32)
    perturb = adv_init * init_noise
    embedded = tokens.astype(jnp.float32) + perturb
    emb_local = embedded.astype(jnp.bfloat16)
    emb_bf = gathered_features(emb_local)
    lefts_in, rights_in, lefts_out, rights_out = [], [], [], []
    for ascent in range(ASCENTS):
        last = ascent + 1 == ASCENTS
        emb = lax.optimization_barrier(emb_bf).astype(jnp.float32)
        inv_rms = lax.rsqrt(jnp.mean(emb * emb, axis=1, keepdims=True) + 1e-06)
        normed = (emb * inv_rms * norm_gain).astype(jnp.bfloat16)
        preact = jnp.dot(normed, weight_in, preferred_element_type=jnp.float32)
        hidden, slope = gelu_and_slope(preact)
        partial_value = jnp.dot(hidden, weight_out, preferred_element_type=jnp.float32)
        mixed = over_tensor(feature_blocks(partial_value.astype(jnp.bfloat16)))
        rights_out += [hidden, from_partner(hidden, "core")]
        lefts_in += for_both_cores(normed, orders)
        out_grad = (embedded + mixed - target) * loss_scale
        grad = gathered_features(out_grad.astype(jnp.bfloat16))
        lefts_out += for_both_cores(grad, orders)
        if last:
            partial_out = partial_over_chip(lefts_out, rights_out)
            slope = slope + nothing(partial_out[:local_tokens])
        hidden_grad = (
            jnp.dot(grad, weight_out.T, preferred_element_type=jnp.float32) * slope
        ).astype(jnp.bfloat16)
        rights_in += [hidden_grad, from_partner(hidden_grad, "core")]
        if not last:
            normed_partial = jnp.dot(hidden_grad, weight_in.T, preferred_element_type=jnp.float32)
            dot_partial = jnp.sum(normed_partial * norm_gain * emb, axis=1)
            dot_head = dot_partial.astype(jnp.bfloat16)
            dot_rest = (dot_partial - dot_head.astype(jnp.float32)).astype(jnp.bfloat16)
            dots = jnp.stack([dot_head, dot_rest], 1)[None]
            blocks = jnp.concatenate(
                [
                    feature_blocks(normed_partial.astype(jnp.bfloat16)),
                    jnp.broadcast_to(dots, (lax.axis_size(TENSOR), local_tokens, 2)),
                ],
                axis=2,
            )
            arrived = over_tensor(blocks)
            scaled = arrived[:, :width_local] * gain_local
            row_dot = jnp.sum(arrived[:, width_local:], axis=1, keepdims=True)
            emb_local = emb_local.astype(jnp.float32)
            delta_grad = (
                out_grad + inv_rms * scaled - emb_local * inv_rms * inv_rms * inv_rms * row_dot / D
            )
            delta_whole = gathered_features(delta_grad.astype(jnp.bfloat16)).astype(jnp.float32)
            row_squares = jnp.sum(delta_whole * delta_whole, axis=1)
            sums = jnp.stack(
                [jnp.sum(onehot * row_squares[:, None], axis=0), jnp.sum(onehot, axis=0)]
            )
            square_sums, counts = over_neighbours(sums)
            root_mean = jnp.sqrt(square_sums / (jnp.maximum(counts, 1.0) * D) + 1e-06)
            token_scale = jnp.sum(onehot * (adv_step / root_mean)[None, :], axis=1)[:, None]
            perturb = perturb + delta_grad * token_scale
            embedded = tokens.astype(jnp.float32) + perturb
            emb_bf = (emb + delta_whole * token_scale).astype(jnp.bfloat16)
    partial_in = partial_over_chip(lefts_in, rights_in)
    sent_out, sent_in = first_step(partial_out, True), first_step(partial_in, False)
    there = [nothing(message) for message in sent_in]
    sums_out = second_step(partial_out, *sent_out, there, True)
    sums_in = second_step(partial_in, *sent_in, (0.0, 0.0), False)
    summed_out, there = over_z(sums_out, 0.0)
    summed_in, _ = over_z(sums_in, there)
    summed_out = summed_out.T
    dp_rows = moment_in.shape[0]
    offset = lax.axis_index(DP) * dp_rows
    own_in = lax.dynamic_slice_in_dim(weight_in, offset, dp_rows, 0)
    own_out = lax.dynamic_slice_in_dim(weight_out, offset, dp_rows, 1)
    new_moment_in = decay * moment_in + summed_in / ASCENTS
    new_moment_out = decay * moment_out + summed_out / ASCENTS
    new_weight_in = (own_in.astype(jnp.float32) - learn_rate * new_moment_in).astype(jnp.bfloat16)
    new_weight_out = (own_out.astype(jnp.float32) - learn_rate * new_moment_out).astype(
        jnp.bfloat16
    )
    return (new_weight_in, new_weight_out, new_moment_in, new_moment_out, perturb)


def solution(mesh):
    torus = Mesh(mesh.devices.reshape(2, 4, 2, 4, 4), DP + TENSOR)
    in_specs = (
        P(DP, TENSOR),
        P(DP, TENSOR),
        P(DP),
        P(DP, TENSOR),
        P(),
        P(None, TENSOR),
        P(TENSOR, None),
        P(DP, TENSOR),
        P(TENSOR, DP),
    )
    out_specs = (P(DP, TENSOR), P(TENSOR, DP), P(DP, TENSOR), P(TENSOR, DP), P(DP, TENSOR))
    return jax.shard_map(
        shards, mesh=torus, in_specs=in_specs, out_specs=out_specs, check_vma=False
    )
```
